256 devices in a mesh: ctx: 32 (over z, y_hi, core), tp: 8 (over x, y_lo).
Axes of the slice: x: 4, y: 4 (y_hi: 2, y_lo: 2; y = y_hi * 2 + y_lo), z: 8, core: 2. Of those that a mesh axis runs over, the one named last changes fastest.
Arguments:
- queries: bfloat16 [64, 2, 8192], P('ctx', None, 'tp'), may hold values from -60 to 60
- new_keys: bfloat16 [2, 64, 1024], P(None, 'ctx', 'tp'), may hold values from -9.5625 to 9.5625
- new_values: bfloat16 [2, 64, 1024], P(None, 'ctx', 'tp'), may hold values from -6 to 6
- cache_keys: bfloat16 [2, 131072, 1024], P(None, 'ctx', 'tp'), may hold values from -6 to 6
- cache_values: bfloat16 [2, 131072, 1024], P(None, 'ctx', 'tp'), may hold values from -6 to 6
- hist_len: int32 [2], replicated, may hold values from 32768 to 122880, as said below
- page_owner: int32 [2, 32], replicated, may hold values from 0 to 31, as said below
- out_weight: bfloat16 [8192, 8192], P('tp', 'ctx'), may hold values from -0.0625 to 0.0625
Outputs:
- attended: bfloat16 [64, 2, 8192], P('tp', None, 'ctx')
- stored_keys: bfloat16 [32, 2, 2, 1024], P('ctx', None, None, 'tp')
- stored_values: bfloat16 [32, 2, 2, 1024], P('ctx', None, None, 'tp')
The draws below stay inside these ranges and needn't reach their ends.
Inputs may be any that keep to these rules, and one draw needn't show every extreme that they name: `hist_len`: some request has the full length. `page_owner`: each row lists every device once; page b of request r holds its new-turn tokens b * 2 to (b + 1) * 2 - 1; some column b holds one value in every row.
All inputs are finite; a program needn't handle non-finite values.
Results may differ from the reference program's by a relative error of at most 0.0085.
Values may be sent and summed in bfloat16 or wider, within the bound.
A program may use at most 64 MiB of HBM per device.

```python
import math
import jax
import jax.numpy as jnp
from jax import lax

D = 8192
H = 64
KVH = 8
HD = 128
REQS = 2
TURN = 64
HDEV = 4096
HIST_CAP = 131072
BLOCKS = 32
PAGE = 2


def drawn_pair(key):
    base = jax.random.fold_in(key, 11)
    key_query, key_cache = jax.random.split(base, 2)
    query = 3.0 * jax.random.truncated_normal(key_query, -6.0, 6.0, (TURN, REQS, H * HD), jnp.float32)
    cache = jax.random.truncated_normal(key_cache, -6.0, 6.0, (REQS, HIST_CAP, KVH * HD), jnp.float32)
    return (query, cache)


def draw_queries(key, part):
    return drawn_pair(key)[0].astype(jnp.bfloat16)


def draw_cache_keys(key, part):
    return drawn_pair(key)[1].astype(jnp.bfloat16)


def draw_hist_len(key, part):
    length_key = jax.random.fold_in(key, 23)
    first_key, second_key = jax.random.split(length_key, 2)
    longest = HIST_CAP - HIST_CAP // 16
    lengths = jax.random.randint(first_key, (REQS,), HIST_CAP // 4, longest + 1)
    full_one = jax.random.randint(second_key, (), 0, REQS)
    lengths = lengths.at[full_one].set(longest)
    return lengths.astype(jnp.int32)


def draw_page_owner(key, part):
    base = jax.random.fold_in(key, 37)
    subkeys = jax.random.split(base, REQS + 2)
    sender = jax.random.randint(subkeys[0], (), 0, BLOCKS)
    target = jax.random.randint(subkeys[1], (), 0, BLOCKS)
    table_rows = []
    for number in range(REQS):
        order = jax.random.permutation(subkeys[number + 2], BLOCKS).astype(jnp.int32)
        where_target = jnp.argmax(order == target)
        displaced = order[sender]
        order = order.at[where_target].set(displaced).at[sender].set(target)
        table_rows.append(order)
    return jnp.stack(table_rows).astype(jnp.int32)


def block_scale(rng, dims, shards, low, high):
    factor_of = 1.0
    for dim, parts in shards:
        steps = jax.random.uniform(jax.random.fold_in(jax.random.fold_in(rng, 6), dim), (parts,), jnp.float32, low / len(shards), high / len(shards))
        factor_of = factor_of * jnp.repeat(jnp.exp(steps), dims[dim] // parts).reshape((-1,) + (1,) * (len(dims) - 1 - dim))
    return factor_of


def scatter_about(stream_key, extent, scale, reach, cuts=(), held_as=jnp.bfloat16):
    values = scale * jax.random.normal(stream_key, extent, jnp.float32)
    if cuts:
        values = values * block_scale(stream_key, extent, cuts, -0.22, 0.18)
    return jnp.clip(values, -reach, reach).astype(held_as)


def setup_inputs(seed: int = 0) -> dict:
    key_list = jax.random.split(jax.random.key(seed), 9)
    return {
        "queries": draw_queries(jax.random.fold_in(key_list[8], 71), 0),
        "new_keys": scatter_about(key_list[1], (REQS, TURN, KVH * HD), 1.6, 9.5625, ((1, 32), (2, 8))),
        "new_values": scatter_about(key_list[2], (REQS, TURN, KVH * HD), 1.0, 6.0, ((1, 32), (2, 8))),
        "cache_keys": draw_cache_keys(jax.random.fold_in(key_list[8], 71), 0),
        "cache_values": scatter_about(key_list[4], (REQS, HIST_CAP, KVH * HD), 1.0, 6.0, ((1, 32), (2, 8))),
        "hist_len": draw_hist_len(jax.random.fold_in(key_list[8], 71), 0),
        "page_owner": draw_page_owner(jax.random.fold_in(key_list[8], 71), 0),
        "out_weight": scatter_about(key_list[7], (H * HD, D), (H * HD) ** -0.5, 0.0625, ((0, 8), (1, 32))),
    }


def slot_positions():
    slots = jnp.arange(HIST_CAP, dtype=jnp.int32)
    device = slots // HDEV
    within = slots % HDEV
    half_size = HDEV // 2
    members = HIST_CAP // HDEV
    return jnp.where(within < half_size, device * half_size + within, (2 * members - 1 - device) * half_size + within - half_size).astype(jnp.int32)

def one_head(query_rows, hist_keys, hist_values, turn_keys, turn_values, visible):
    group_size = query_rows.shape[1]
    flattened = query_rows.reshape(TURN * group_size, HD)
    keys_all = jnp.concatenate([hist_keys, turn_keys], axis=0)
    values_all = jnp.concatenate([hist_values, turn_values], axis=0)
    scores = jnp.dot(flattened, keys_all.T, preferred_element_type=jnp.float32) * (1.0 / math.sqrt(HD))
    scores = scores.reshape(TURN, group_size, keys_all.shape[0])
    counted = visible[:, None, :]
    peak = lax.optimization_barrier(jnp.max(jnp.where(counted, scores, -jnp.inf), axis=-1, keepdims=True))
    weights = jnp.where(counted, jnp.exp(scores - peak), 0.0)
    total = lax.optimization_barrier(jnp.sum(weights, axis=-1))
    probs = weights.astype(jnp.bfloat16).reshape(TURN * group_size, keys_all.shape[0])
    summed = jnp.dot(probs, values_all, preferred_element_type=jnp.float32).reshape(TURN, group_size, HD)
    return summed / total[..., None]

def reference(queries, new_keys, new_values, cache_keys, cache_values, hist_len, page_owner, out_weight):
    group_size = H // KVH
    position = slot_positions()
    turn_steps = jnp.arange(TURN, dtype=jnp.int32)
    causal = turn_steps[None, :] <= turn_steps[:, None]

    def per_request(request):
        live = position < hist_len[request]
        visible = jnp.concatenate([jnp.broadcast_to(live[None, :], (TURN, HIST_CAP)), causal], axis=1)
        query_req = queries[:, request, :].reshape(TURN, KVH, group_size, HD)
        hist_k = cache_keys[request]
        hist_v = cache_values[request]
        turn_k = new_keys[request]
        turn_v = new_values[request]

        def per_head(head):
            offset = (head * HD).astype(jnp.int32)
            return one_head(lax.dynamic_index_in_dim(query_req, head, 1, keepdims=False), lax.dynamic_slice_in_dim(hist_k, offset, HD, 1), lax.dynamic_slice_in_dim(hist_v, offset, HD, 1), lax.dynamic_slice_in_dim(turn_k, offset, HD, 1), lax.dynamic_slice_in_dim(turn_v, offset, HD, 1), visible)
        heads = lax.map(per_head, jnp.arange(KVH, dtype=jnp.int32))
        return jnp.transpose(heads, (1, 0, 2, 3)).reshape(TURN, H * HD)
    outputs = lax.map(per_request, jnp.arange(REQS, dtype=jnp.int32))
    attention = jnp.transpose(outputs, (1, 0, 2)).astype(jnp.bfloat16)
    attended = jnp.dot(attention.reshape(TURN * REQS, H * HD), out_weight, preferred_element_type=jnp.float32)
    attended = attended.astype(jnp.bfloat16).reshape(TURN, REQS, D)
    owners = jnp.arange(BLOCKS, dtype=jnp.int32)
    matches = (page_owner[None, :, :] == owners[:, None, None]).astype(jnp.int32)
    source = lax.optimization_barrier(jnp.sum(matches * owners[None, None, :], axis=2)).astype(jnp.int32)
    request_ids = jnp.broadcast_to(jnp.arange(REQS, dtype=jnp.int32)[None, :], (BLOCKS, REQS))
    pages_keys = new_keys.reshape(REQS, BLOCKS, PAGE, KVH * HD)
    pages_values = new_values.reshape(REQS, BLOCKS, PAGE, KVH * HD)
    stored_keys = pages_keys[request_ids, source]
    stored_values = pages_values[request_ids, source]
    return (attended, stored_keys, stored_values)
```

```python
import functools
import math

import jax
import jax.numpy as jnp
from jax import lax
from jax.experimental import pallas as pl
from jax.experimental.pallas import tpu as pltpu
from jax.sharding import PartitionSpec as P

HD = 128
FLOOR = -1e30
KEY_BLOCK = 512
MESH = pl.DeviceIdType.MESH


def kernel(
    members,
    groups,
    q_ref,
    nk_ref,
    nv_ref,
    ck_ref,
    cv_ref,
    hist_ref,
    owner_ref,
    w_ref,
    out_ref,
    sk_ref,
    sv_ref,
    kbuf,
    vbuf,
    wbuf,
    qtmp,
    ktail,
    qall,
    kvall,
    scores,
    acc,
    ready,
    lse,
    osend,
    lsend,
    orecv,
    lrecv,
    abuf,
    psend,
    precv,
    load_sem,
    qs_sem,
    qr_sem,
    ks_sem,
    kr_sem,
    os_sem,
    or_sem,
    ls_sem,
    lr_sem,
    as_sem,
    ar_sem,
    ps_sem,
    pr_sem,
):
    me = lax.axis_index("ctx")
    mine = lax.axis_index("tp")
    requests, history = ck_ref.shape[:2]
    page = q_ref.shape[0]
    heads = q_ref.shape[2] // HD
    turn = page * members
    rows = turn * heads
    half_size = history // 2
    tail = kbuf.shape[1] - history
    factor = math.log2(math.e) / math.sqrt(HD)

    def load(r):
        return (
            pltpu.make_async_copy(ck_ref.at[r], kbuf.at[r, pl.ds(0, history)], load_sem.at[2 * r]),
            pltpu.make_async_copy(cv_ref.at[r], vbuf.at[r, pl.ds(0, history)], load_sem.at[2 * r + 1]),
        )

    load_w = pltpu.make_async_copy(w_ref, wbuf, load_sem.at[2 * requests])
    for r in range(requests):
        for copy in load(r):
            copy.start()
    load_w.start()

    barrier = pltpu.get_barrier_semaphore()

    def greet(axis, size, position):
        def one(k, c):
            pl.semaphore_signal(
                barrier, inc=1, device_id={axis: lax.rem(position + k, size)}, device_id_type=MESH
            )
            return c

        lax.fori_loop(1, size, one, 0)

    greet("ctx", members, me)
    greet("tp", groups, mine)

    for t in range(page):
        row = q_ref[t].astype(jnp.float32)
        for h in range(heads):
            for r in range(requests):
                qtmp[r, pl.ds(t * heads + h, 1), :] = row[r : r + 1, h * HD : (h + 1) * HD]
    qall[me] = qtmp[...].astype(qall.dtype)
    kvall[me, 0] = nk_ref[...]
    kvall[me, 1] = nv_ref[...]
    pl.semaphore_wait(barrier, members - 1 + groups - 1)

    def to(k):
        return lax.rem(me + k, members)

    def query_copy(r, source, target):
        return pltpu.make_async_remote_copy(
            src_ref=qall.at[source, r],
            dst_ref=qall.at[source, r],
            send_sem=qs_sem.at[r, target],
            recv_sem=qr_sem.at[r, source],
            device_id={"ctx": target},
            device_id_type=MESH,
        )

    def page_copy(source, target):
        return pltpu.make_async_remote_copy(
            src_ref=kvall.at[source],
            dst_ref=kvall.at[source],
            send_sem=ks_sem.at[target],
            recv_sem=kr_sem.at[source],
            device_id={"ctx": target},
            device_id_type=MESH,
        )

    def for_peers(fn):
        def one(k, c):
            fn(to(k))
            return c

        lax.fori_loop(1, members, one, 0)

    for r in range(requests):
        for_peers(lambda peer: query_copy(r, me, peer).start())
    for_peers(lambda peer: page_copy(me, peer).start())

    for r in range(requests):
        for source, target in ((nk_ref, kbuf), (nv_ref, vbuf)):
            ktail[...] = jnp.zeros_like(ktail)
            ktail[pl.ds(0, page), :] = source[r].astype(jnp.float32)
            target[r, pl.ds(history, tail), :] = ktail[...].astype(target.dtype)

    ones = jnp.ones((KEY_BLOCK, HD), jnp.bfloat16)
    row_token = lax.broadcasted_iota(jnp.int32, (rows, tail), 0) // heads
    tail_lane = lax.broadcasted_iota(jnp.int32, (rows, tail), 1)
    tail_visible = (tail_lane < page) & (tail_lane + page * me <= row_token)
    token_row = lax.broadcasted_iota(jnp.int32, (turn // 2, HD), 0)
    token_lane = lax.broadcasted_iota(jnp.int32, (turn // 2, HD), 1)

    def piece_copy(source, target):
        return (
            pltpu.make_async_remote_copy(
                src_ref=osend.at[target],
                dst_ref=orecv.at[source],
                send_sem=os_sem.at[target],
                recv_sem=or_sem.at[source],
                device_id={"ctx": target},
                device_id_type=MESH,
            ),
            pltpu.make_async_remote_copy(
                src_ref=lsend.at[target],
                dst_ref=lrecv.at[source],
                send_sem=ls_sem.at[target],
                recv_sem=lr_sem.at[source],
                device_id={"ctx": target},
                device_id_type=MESH,
            ),
        )

    dot_nt = functools.partial(
        lax.dot_general,
        dimension_numbers=(((1,), (1,)), ((), ())),
        preferred_element_type=jnp.float32,
    )
    for r in range(requests):
        for copy in load(r):
            copy.wait()
        for_peers(lambda peer: query_copy(r, peer, me).wait_recv())
        queries = qall[:, r].reshape(rows, HD)

        def score(b, peak):
            offset = pl.multiple_of(b * KEY_BLOCK, KEY_BLOCK)
            block = dot_nt(queries, kbuf[r, pl.ds(offset, KEY_BLOCK), :])
            first = jnp.where(
                offset < half_size,
                me * half_size + offset,
                (2 * members - 1 - me) * half_size + offset - half_size,
            )
            lane = lax.broadcasted_iota(jnp.int32, (1, KEY_BLOCK), 1)
            block = block + jnp.where(lane < hist_ref[r] - first, 0.0, FLOOR)
            scores[:, pl.ds(offset, KEY_BLOCK)] = block
            for p in range(KEY_BLOCK // HD):
                peak = jnp.maximum(peak, block[:, p * HD : (p + 1) * HD])
            return peak

        last = dot_nt(queries, kbuf[r, pl.ds(history, tail), :])
        last = jnp.where(tail_visible, last, FLOOR)
        acc_peak = lax.fori_loop(0, history // KEY_BLOCK, score, last)
        peak = jnp.max(acc_peak, axis=1, keepdims=True)

        weights = jnp.exp2((last - peak) * factor).astype(jnp.bfloat16)
        values = jnp.concatenate([vbuf[r, pl.ds(history, tail), :], ones[:tail]], axis=1)
        acc[...] = jnp.dot(weights, values, preferred_element_type=jnp.float32)

        def add(b, c):
            offset = pl.multiple_of(b * KEY_BLOCK, KEY_BLOCK)
            weights = jnp.exp2((scores[:, pl.ds(offset, KEY_BLOCK)] - peak) * factor).astype(jnp.bfloat16)
            values = jnp.concatenate([vbuf[r, pl.ds(offset, KEY_BLOCK), :], ones], axis=1)
            acc[...] += jnp.dot(weights, values, preferred_element_type=jnp.float32)
            return c

        lax.fori_loop(0, history // KEY_BLOCK, add, 0)
        total = acc[:, HD:]
        lse[...] = peak * factor + jnp.log2(total)
        ready[...] = acc[:, :HD] / total

        for h in range(heads):
            for half in range(2):
                target = h * 4 + half * 2 + r
                picked = pl.ds(half * (turn // 2) * heads + h, turn // 2, stride=heads)
                osend[target] = ready[picked, :].astype(osend.dtype)
                lsend[target] = jnp.sum(
                    jnp.where(token_row == token_lane, lse[picked, :], 0.0), axis=0, keepdims=True
                )

        def send(k, c):
            target = lax.rem((me // requests) + k, members // requests) * requests + r

            @pl.when(target != me)
            def _():
                for copy in piece_copy(me, target):
                    copy.start()

            return c

        lax.fori_loop(0, members // requests, send, 0)

    orecv[me] = osend[me]
    lrecv[me] = lsend[me]

    def arrived(peer):
        for copy in piece_copy(peer, me):
            copy.wait_recv()

    for_peers(arrived)
    levels = lrecv[...].reshape(members, HD)
    levels = jnp.concatenate([levels, jnp.full((HD - members, HD), FLOOR, jnp.float32)], axis=0)
    levels = levels.T[: turn // 2]
    share = jnp.exp2(levels - jnp.max(levels, axis=1, keepdims=True))
    share = share / jnp.sum(share, axis=1, keepdims=True)
    done = jnp.zeros((turn // 2, HD), jnp.float32)
    for s in range(members):
        done = done + share[:, s : s + 1] * orecv[s].astype(jnp.float32)
    head = me // 4
    first_row = pl.multiple_of((lax.rem(me, 2) * 2 + lax.rem(me // 2, 2)) * (turn // 2), turn // 2)
    abuf[head, pl.ds(first_row, turn // 2), :] = done.astype(abuf.dtype)

    def finished_copy(source, target):
        start = pl.multiple_of((lax.rem(source, 2) * 2 + lax.rem(source // 2, 2)) * (turn // 2), turn // 2)
        place = abuf.at[source // 4, pl.ds(start, turn // 2)]
        return pltpu.make_async_remote_copy(
            src_ref=place,
            dst_ref=place,
            send_sem=as_sem.at[target],
            recv_sem=ar_sem.at[source],
            device_id={"ctx": target},
            device_id_type=MESH,
        )

    for_peers(lambda peer: finished_copy(me, peer).start())
    load_w.wait()
    for_peers(lambda peer: page_copy(peer, me).wait_recv())
    for r in range(requests):
        source = jnp.int32(0)
        for b in range(members):
            source = jnp.maximum(source, jnp.where(owner_ref[r, b] == me, b, 0))
        sk_ref[r] = kvall[source, 0, r]
        sv_ref[r] = kvall[source, 1, r]
    for_peers(lambda peer: finished_copy(peer, me).wait_recv())

    rows_in = jnp.concatenate([abuf[h] for h in range(heads)], axis=1)
    part = jnp.dot(rows_in, wbuf[...], preferred_element_type=jnp.float32)
    share_rows = turn // groups
    for g in range(groups):
        psend[g] = jnp.concatenate(
            [part[r * turn + g * share_rows : r * turn + (g + 1) * share_rows] for r in range(requests)], axis=0
        ).astype(psend.dtype)

    def part_copy(source, target):
        return pltpu.make_async_remote_copy(
            src_ref=psend.at[target],
            dst_ref=precv.at[source],
            send_sem=ps_sem.at[target],
            recv_sem=pr_sem.at[source],
            device_id={"tp": target},
            device_id_type=MESH,
        )

    def for_groups(fn):
        def one(k, c):
            fn(lax.rem(mine + k, groups))
            return c

        lax.fori_loop(1, groups, one, 0)

    for_groups(lambda peer: part_copy(mine, peer).start())
    precv[mine] = psend[mine]
    for_groups(lambda peer: part_copy(peer, mine).wait_recv())
    full = precv[0].astype(jnp.float32)
    for g in range(1, groups):
        full = full + precv[g].astype(jnp.float32)
    out_ref[...] = full

    def drained(peer):
        for r in range(requests):
            query_copy(r, me, peer).wait_send()
        page_copy(me, peer).wait_send()
        for copy in piece_copy(me, peer):
            copy.wait_send()
        finished_copy(me, peer).wait_send()

    for_peers(drained)
    for_groups(lambda peer: part_copy(mine, peer).wait_send())


def on_device(queries, new_keys, new_values, cache_keys, cache_values, hist_len, page_owner, out_weight):
    members = lax.axis_size("ctx")
    groups = lax.axis_size("tp")
    page, requests, width = queries.shape
    history = cache_keys.shape[1]
    heads = width // HD
    turn = page * members
    columns = out_weight.shape[1]
    vmem = pl.BlockSpec(memory_space=pltpu.VMEM)
    smem = pl.BlockSpec(memory_space=pltpu.SMEM)
    anywhere = pl.BlockSpec(memory_space=pl.ANY)
    bf16, f32 = jnp.bfloat16, jnp.float32
    dma = pltpu.SemaphoreType.DMA
    full, kept_keys, kept_values = pl.pallas_call(
        functools.partial(kernel, members, groups),
        out_shape=(
            jax.ShapeDtypeStruct((requests * (turn // groups), columns), f32),
            jax.ShapeDtypeStruct(new_keys.shape, bf16),
            jax.ShapeDtypeStruct(new_keys.shape, bf16),
        ),
        in_specs=[vmem, vmem, vmem, anywhere, anywhere, smem, smem, anywhere],
        out_specs=[vmem, vmem, vmem],
        scratch_shapes=[
            pltpu.VMEM((requests, history + HD, HD), bf16),
            pltpu.VMEM((requests, history + HD, HD), bf16),
            pltpu.VMEM(out_weight.shape, bf16),
            pltpu.VMEM((requests, page * heads, HD), f32),
            pltpu.VMEM((HD, HD), f32),
            pltpu.VMEM((members, requests, page * heads, HD), bf16),
            pltpu.VMEM((members, 2, *new_keys.shape), bf16),
            pltpu.VMEM((turn * heads, history), f32),
            pltpu.VMEM((turn * heads, 2 * HD), f32),
            pltpu.VMEM((turn * heads, HD), f32),
            pltpu.VMEM((turn * heads, HD), f32),
            pltpu.VMEM((members, turn // 2, HD), bf16),
            pltpu.VMEM((members, 1, HD), f32),
            pltpu.VMEM((members, turn // 2, HD), bf16),
            pltpu.VMEM((members, 1, HD), f32),
            pltpu.VMEM((heads, requests * turn, HD), bf16),
            pltpu.VMEM((groups, requests * (turn // groups), columns), bf16),
            pltpu.VMEM((groups, requests * (turn // groups), columns), bf16),
            dma((2 * requests + 1,)),
            dma((requests, members)),
            dma((requests, members)),
            dma((members,)),
            dma((members,)),
            dma((members,)),
            dma((members,)),
            dma((members,)),
            dma((members,)),
            dma((members,)),
            dma((members,)),
            dma((groups,)),
            dma((groups,)),
        ],
        compiler_params=pltpu.CompilerParams(collective_id=0, has_side_effects=True),
    )(queries, new_keys, new_values, cache_keys, cache_values, hist_len, page_owner, out_weight)
    attended = full.astype(bf16).reshape(requests, turn // groups, columns).transpose(1, 0, 2)
    return (attended, kept_keys[None], kept_values[None])


def solution(mesh):
    return jax.shard_map(
        on_device,
        mesh=mesh,
        in_specs=(
            P("ctx", None, "tp"),
            P(None, "ctx", "tp"),
            P(None, "ctx", "tp"),
            P(None, "ctx", "tp"),
            P(None, "ctx", "tp"),
            P(),
            P(),
            P("tp", "ctx"),
        ),
        out_specs=(P("tp", None, "ctx"), P("ctx", None, None, "tp"), P("ctx", None, None, "tp")),
        check_vma=False,
    )
```

```python
import functools
import math

import jax
import jax.numpy as jnp
from jax import lax
from jax.experimental import pallas as pl
from jax.experimental.pallas import tpu as pltpu
from jax.sharding import PartitionSpec as P

HD = 128
FLOOR = -1e30
MESH = pl.DeviceIdType.MESH


def kernel(
    members,
    groups,
    q_ref,
    nk_ref,
    nv_ref,
    ck_ref,
    cv_ref,
    hist_ref,
    owner_ref,
    w_ref,
    out_ref,
    sk_ref,
    sv_ref,
    kbuf,
    vbuf,
    wbuf,
    qtmp,
    ktail,
    qown,
    qall,
    kvall,
    scores,
    acc,
    ready,
    lse,
    osend,
    lsend,
    orecv,
    lrecv,
    abuf,
    psend,
    precv,
    load_sem,
    chip_send,
    chip_recv,
    q_send,
    q_recv,
    page_send,
    page_recv,
    o_send,
    o_recv,
    l_send,
    l_recv,
    f_send,
    f_recv,
    p_send,
    p_recv,
):
    me = lax.axis_index("ctx")
    mine = lax.axis_index("tp")
    requests, history = ck_ref.shape[:2]
    page = q_ref.shape[0]
    heads = q_ref.shape[2] // HD
    turn = page * members
    chunk = turn // 2
    rows = chunk * heads
    half_size = history // 2
    owners = members // requests
    near = members // 2
    share_rows = turn // groups
    tail = kbuf.shape[0] - 2 * history
    factor = math.log2(math.e) / math.sqrt(HD)

    r = lax.rem(me, 2)
    other = 1 - r
    partner = me + 1 - 2 * r
    own = me // 2
    side = own // heads

    load_k = pltpu.make_async_copy(ck_ref.at[r], kbuf.at[pl.ds(0, history)], load_sem.at[0])
    load_v = pltpu.make_async_copy(cv_ref.at[r], vbuf.at[pl.ds(0, history)], load_sem.at[1])
    load_w = pltpu.make_async_copy(w_ref, wbuf.at[r], load_sem.at[2])
    load_k.start()
    load_v.start()
    load_w.start()

    barrier = pltpu.get_barrier_semaphore()

    def greet(**device):
        pl.semaphore_signal(barrier, inc=1, device_id=device, device_id_type=MESH)

    def greet_ctx(k, c):
        greet(ctx=lax.rem(me + k, members))
        return c

    def greet_tp(k, c):
        for j in range(requests):
            greet(ctx=me - r + j, tp=lax.rem(mine + k, groups))
        return c

    lax.fori_loop(1, members, greet_ctx, 0)
    lax.fori_loop(1, groups, greet_tp, 0)

    for t in range(page):
        row = q_ref[t].astype(jnp.float32)
        for h in range(heads):
            for s in range(requests):
                qtmp[s, pl.ds(t * heads + h, 1), :] = row[s : s + 1, h * HD : (h + 1) * HD]
    qown[...] = qtmp[...].astype(qown.dtype)
    qall[me] = qown[r]
    kvall[me, 0] = nk_ref[...]
    kvall[me, 1] = nv_ref[...]
    pl.semaphore_wait(barrier, members - 1 + requests * (groups - 1))

    def remote(src, dst, send_sem, recv_sem, **device):
        return pltpu.make_async_remote_copy(
            src_ref=src, dst_ref=dst, send_sem=send_sem, recv_sem=recv_sem, device_id=device, device_id_type=MESH
        )

    def landed(ref, sem):
        pltpu.make_async_copy(ref, ref, sem).wait()

    def send_query(peer, where):
        remote(qown.at[lax.rem(peer, 2)], qall.at[me], q_send, q_recv.at[where], ctx=peer).start()

    def near_query(k, c):
        send_query(side * near + lax.rem(lax.rem(me, near) + k, near), 0)
        return c

    def far_query(k, c):
        send_query((1 - side) * near + lax.rem(lax.rem(me, near) + k, near), 1)
        return c

    lax.fori_loop(1, near, near_query, 0)
    lax.fori_loop(0, near, far_query, 0)

    history_slab = pl.ds(history, history)
    give_k = remote(ck_ref.at[other], kbuf.at[history_slab], chip_send.at[0], chip_recv.at[0], ctx=partner)
    give_v = remote(cv_ref.at[other], vbuf.at[history_slab], chip_send.at[1], chip_recv.at[1], ctx=partner)
    give_w = remote(w_ref, wbuf.at[r], chip_send.at[2], chip_recv.at[2], ctx=partner)
    give_page = remote(kvall.at[me], kvall.at[me], chip_send.at[3], chip_recv.at[3], ctx=partner)
    give_page.start()
    give_k.start()
    give_v.start()
    give_w.start()

    give_page.wait_recv()
    for source, target in ((0, kbuf), (1, vbuf)):
        ktail[...] = jnp.zeros_like(ktail)
        for j in range(2):
            ktail[pl.ds(j * page, page), :] = kvall[me - r + j, source, r].astype(jnp.float32)
        target[pl.ds(2 * history, tail), :] = ktail[...].astype(target.dtype)

    ones = jnp.ones((history, HD), jnp.bfloat16)
    row_token = lax.broadcasted_iota(jnp.int32, (rows, tail), 0) // heads
    tail_lane = lax.broadcasted_iota(jnp.int32, (rows, tail), 1)
    token_row = lax.broadcasted_iota(jnp.int32, (chunk, HD), 0)
    token_lane = lax.broadcasted_iota(jnp.int32, (chunk, HD), 1)
    slot = lax.broadcasted_iota(jnp.int32, (1, history), 1)

    def bias_of(device):
        low = hist_ref[r] - device * half_size
        high = hist_ref[r] - (2 * members - 1 - device) * half_size + half_size
        return jnp.where(slot < jnp.where(slot < half_size, low, high), 0.0, FLOOR)

    dot_nt = functools.partial(
        lax.dot_general,
        dimension_numbers=(((1,), (1,)), ((), ())),
        preferred_element_type=jnp.float32,
    )

    def score(queries, b, device, peak):
        block = dot_nt(queries, kbuf[b * history : (b + 1) * history, :]) + bias_of(device)
        scores[:, b * history : (b + 1) * history] = block
        for p in range(history // HD):
            peak = jnp.maximum(peak, block[:, p * HD : (p + 1) * HD])
        return peak

    def weigh(b, peak):
        weights = jnp.exp2((scores[:, b * history : (b + 1) * history] - peak) * factor).astype(jnp.bfloat16)
        values = jnp.concatenate([vbuf[b * history : (b + 1) * history, :], ones], axis=1)
        return jnp.dot(weights, values, preferred_element_type=jnp.float32)

    for turn_half in range(2):
        which = side if turn_half == 0 else 1 - side
        first = which * near
        if turn_half == 0:
            landed(qall.at[pl.ds(0, near - 1)], q_recv.at[0])
            load_k.wait()
        else:
            landed(qall.at[pl.ds(0, near)], q_recv.at[1])
        queries = qall[pl.ds(first, near)].reshape(rows, HD)
        last = dot_nt(queries, kbuf[2 * history :, :])
        visible = (tail_lane < 2 * page) & (tail_lane + 2 * page * own <= row_token + which * chunk)
        last = jnp.where(visible, last, FLOOR)
        peak = score(queries, 0, me, last)
        if turn_half == 0:
            give_k.wait_recv()
        peak = score(queries, 1, partner, peak)
        peak = jnp.max(peak, axis=1, keepdims=True)
        weights = jnp.exp2((last - peak) * factor).astype(jnp.bfloat16)
        values = jnp.concatenate([vbuf[2 * history :, :], ones[:tail]], axis=1)
        acc[...] = jnp.dot(weights, values, preferred_element_type=jnp.float32)
        if turn_half == 0:
            load_v.wait()
        acc[...] += weigh(0, peak)
        if turn_half == 0:
            give_v.wait_recv()
        acc[...] += weigh(1, peak)
        total = acc[:, HD:]
        lse[...] = peak * factor + jnp.log2(total)
        ready[...] = acc[:, :HD] / total

        base = (1 - which) * heads
        for h in range(heads):
            picked = pl.ds(h, chunk, stride=heads)
            osend[base + h] = ready[picked, :].astype(osend.dtype)
            lsend[base + h] = jnp.sum(jnp.where(token_row == token_lane, lse[picked, :], 0.0), axis=0, keepdims=True)

        def send_piece(k, c):
            target = base + lax.rem(k + own, heads)

            @pl.when(target != own)
            def _():
                remote(osend.at[target], orecv.at[own], o_send, o_recv, ctx=requests * target + r).start()
                remote(lsend.at[target], lrecv.at[own], l_send, l_recv, ctx=requests * target + r).start()

            return c

        lax.fori_loop(0, heads, send_piece, 0)

    def send_page(k, c):
        peer = lax.rem(me + k, members)

        @pl.when(peer != partner)
        def _():
            remote(kvall.at[me], kvall.at[me], page_send, page_recv, ctx=peer).start()

        return c

    lax.fori_loop(1, members, send_page, 0)

    orecv[own] = osend[own]
    lrecv[own] = lsend[own]
    landed(lrecv.at[pl.ds(0, owners - 1)], l_recv)
    levels = lrecv[...].reshape(owners, HD)
    levels = jnp.concatenate([levels, jnp.full((HD - owners, HD), FLOOR, jnp.float32)], axis=0)
    levels = levels.T[:chunk]
    share = jnp.exp2(levels - jnp.max(levels, axis=1, keepdims=True))
    share = share / jnp.sum(share, axis=1, keepdims=True)
    landed(orecv.at[pl.ds(0, owners - 1)], o_recv)
    done = jnp.zeros((chunk, HD), jnp.float32)
    for s in range(owners):
        done = done + share[:, s : s + 1] * orecv[s].astype(jnp.float32)
    place = abuf.at[lax.rem(own, heads), pl.ds(pl.multiple_of((1 - side) * chunk, chunk), chunk)]
    place[...] = done.astype(abuf.dtype)

    def send_finished(k, c):
        remote(place, place, f_send, f_recv, ctx=lax.rem(me + requests * k, members)).start()
        return c

    lax.fori_loop(1, owners, send_finished, 0)

    landed(kvall.at[pl.ds(0, members - 2)], page_recv)
    for s in range(requests):
        source = jnp.int32(0)
        for b in range(members):
            source = jnp.maximum(source, jnp.where(owner_ref[s, b] == me, b, 0))
        sk_ref[s] = kvall[source, 0, s]
        sv_ref[s] = kvall[source, 1, s]
    load_w.wait()
    give_w.wait_recv()

    flat = abuf.reshape(owners, chunk, HD)
    landed(flat.at[pl.ds(0, owners - 1)], f_recv)
    rows_in = jnp.concatenate([abuf[h] for h in range(heads)], axis=1)
    for j in range(requests):
        part = jnp.dot(rows_in, wbuf[j], preferred_element_type=jnp.float32).astype(psend.dtype)
        for g in range(groups):
            psend[g, j] = part[g * share_rows : (g + 1) * share_rows]

    def send_part(k, c):
        peer = lax.rem(mine + k, groups)
        for j in range(requests):
            remote(psend.at[peer, j], precv.at[mine, r], p_send, p_recv, ctx=me - r + j, tp=peer).start()
        return c

    lax.fori_loop(1, groups, send_part, 0)
    remote(psend.at[mine, other], precv.at[mine, r], p_send, p_recv, ctx=partner).start()
    precv[mine, r] = psend[mine, r]
    flat_parts = precv.reshape(requests * groups, share_rows, precv.shape[3])
    landed(flat_parts.at[pl.ds(0, requests * groups - 1)], p_recv)
    full = precv[0].astype(jnp.float32)
    for g in range(1, groups):
        full = full + precv[g].astype(jnp.float32)
    out_ref[...] = full

    for give in (give_k, give_v, give_w, give_page):
        give.wait_send()
    landed(qall.at[pl.ds(0, members - 1)], q_send)
    landed(kvall.at[pl.ds(0, members - 2)], page_send)
    landed(orecv.at[pl.ds(0, owners - 1)], o_send)
    landed(lrecv.at[pl.ds(0, owners - 1)], l_send)
    landed(flat.at[pl.ds(0, owners - 1)], f_send)
    landed(flat_parts.at[pl.ds(0, requests * groups - 1)], p_send)


def on_device(queries, new_keys, new_values, cache_keys, cache_values, hist_len, page_owner, out_weight):
    members = lax.axis_size("ctx")
    groups = lax.axis_size("tp")
    page, requests, width = queries.shape
    history = cache_keys.shape[1]
    heads = width // HD
    turn = page * members
    chunk = turn // 2
    owners = members // requests
    share_rows = turn // groups
    columns = out_weight.shape[1]
    vmem = pl.BlockSpec(memory_space=pltpu.VMEM)
    smem = pl.BlockSpec(memory_space=pltpu.SMEM)
    anywhere = pl.BlockSpec(memory_space=pl.ANY)
    bf16, f32 = jnp.bfloat16, jnp.float32
    dma = pltpu.SemaphoreType.DMA
    full, kept_keys, kept_values = pl.pallas_call(
        functools.partial(kernel, members, groups),
        out_shape=(
            jax.ShapeDtypeStruct((requests, share_rows, columns), f32),
            jax.ShapeDtypeStruct(new_keys.shape, bf16),
            jax.ShapeDtypeStruct(new_keys.shape, bf16),
        ),
        in_specs=[vmem, vmem, vmem, anywhere, anywhere, smem, smem, anywhere],
        out_specs=[vmem, vmem, vmem],
        scratch_shapes=[
            pltpu.VMEM((2 * history + HD, HD), bf16),
            pltpu.VMEM((2 * history + HD, HD), bf16),
            pltpu.VMEM((requests, *out_weight.shape), bf16),
            pltpu.VMEM((requests, page * heads, HD), f32),
            pltpu.VMEM((HD, HD), f32),
            pltpu.VMEM((requests, page * heads, HD), bf16),
            pltpu.VMEM((members, page * heads, HD), bf16),
            pltpu.VMEM((members, 2, *new_keys.shape), bf16),
            pltpu.VMEM((chunk * heads, 2 * history), f32),
            pltpu.VMEM((chunk * heads, 2 * HD), f32),
            pltpu.VMEM((chunk * heads, HD), f32),
            pltpu.VMEM((chunk * heads, HD), f32),
            pltpu.VMEM((owners, chunk, HD), bf16),
            pltpu.VMEM((owners, 1, HD), f32),
            pltpu.VMEM((owners, chunk, HD), bf16),
            pltpu.VMEM((owners, 1, HD), f32),
            pltpu.VMEM((heads, turn, HD), bf16),
            pltpu.VMEM((groups, requests, share_rows, columns), bf16),
            pltpu.VMEM((groups, requests, share_rows, columns), bf16),
            dma((3,)),
            dma((4,)),
            dma((4,)),
            dma(()),
            dma((2,)),
            dma(()),
            dma(()),
            dma(()),
            dma(()),
            dma(()),
            dma(()),
            dma(()),
            dma(()),
            dma(()),
            dma(()),
        ],
        compiler_params=pltpu.CompilerParams(collective_id=0, has_side_effects=True),
    )(queries, new_keys, new_values, cache_keys, cache_values, hist_len, page_owner, out_weight)
    attended = full.astype(bf16).transpose(1, 0, 2)
    return (attended, kept_keys[None], kept_values[None])


def solution(mesh):
    return jax.shard_map(
        on_device,
        mesh=mesh,
        in_specs=(
            P("ctx", None, "tp"),
            P(None, "ctx", "tp"),
            P(None, "ctx", "tp"),
            P(None, "ctx", "tp"),
            P(None, "ctx", "tp"),
            P(),
            P(),
            P("tp", "ctx"),
        ),
        out_specs=(P("tp", None, "ctx"), P("ctx", None, None, "tp"), P("ctx", None, None, "tp")),
        check_vma=False,
    )
```

```python
import functools
import math

import jax
import jax.numpy as jnp
from jax import lax
from jax.experimental import pallas as pl
from jax.experimental.pallas import tpu as pltpu
from jax.sharding import PartitionSpec as P

HD = 128
FLOOR = -1e30
KEY_BLOCK = 4096
MESH = pl.DeviceIdType.MESH


def kernel(
    members,
    groups,
    q_ref,
    nk_ref,
    nv_ref,
    ck_ref,
    cv_ref,
    hist_ref,
    owner_ref,
    w_ref,
    out_ref,
    pages_ref,
    kbuf,
    vbuf,
    wbuf,
    qtmp,
    ktail,
    qall,
    kvall,
    scores,
    acc,
    ready,
    lse,
    osend,
    lsend,
    orecv,
    lrecv,
    abuf,
    psend,
    precv,
    load_sem,
    chip_send,
    chip_recv,
    z_send,
    z_recv,
    q_send,
    q_recv,
    page_send,
    page_recv,
    o_send,
    o_recv,
    l_send,
    l_recv,
    f_send,
    f_recv,
    p_send,
    p_recv,
):
    me = lax.axis_index("ctx")
    mine = lax.axis_index("tp")
    requests, history = ck_ref.shape[:2]
    page = q_ref.shape[0]
    heads = q_ref.shape[2] // HD
    turn = page * members
    chunk = turn // 2
    rows = chunk * heads
    half_size = history // 2
    owners = members // requests
    near = members // 2
    share_rows = turn // groups
    tail = kbuf.shape[0] - 2 * history
    factor = math.log2(math.e) / math.sqrt(HD)

    r = lax.rem(me, 2)
    other = 1 - r
    partner = me + 1 - 2 * r
    cell_size = 4
    depth = members // cell_size
    across = me + 2 - 4 * lax.rem(me // 2, 2)
    diagonal = across + 1 - 2 * r
    own = me // 2
    side = own // heads

    load_k = pltpu.make_async_copy(ck_ref.at[r], kbuf.at[pl.ds(0, history)], load_sem.at[0])
    load_v = pltpu.make_async_copy(cv_ref.at[r], vbuf.at[pl.ds(0, history)], load_sem.at[1])
    load_w = pltpu.make_async_copy(w_ref, wbuf.at[r], load_sem.at[2])
    load_k.start()
    load_v.start()
    load_w.start()

    barrier = pltpu.get_barrier_semaphore()

    def greet(**device):
        pl.semaphore_signal(barrier, inc=1, device_id=device, device_id_type=MESH)

    def greet_z(k, c):
        greet(ctx=lax.rem(me + cell_size * k, members))
        return c

    def greet_tp(k, c):
        for j in range(requests):
            greet(ctx=me - r + j, tp=lax.rem(mine + k, groups))
        return c

    lax.fori_loop(1, depth, greet_z, 0)
    for cell in (partner, across, diagonal):
        greet(ctx=cell)
    lax.fori_loop(1, groups, greet_tp, 0)

    for t in range(page):
        row = q_ref[t].astype(jnp.float32)
        for h in range(heads):
            for s in range(requests):
                qtmp[s, pl.ds(t * heads + h, 1), :] = row[s : s + 1, h * HD : (h + 1) * HD]
    qall[me, 0] = qtmp[r].astype(qall.dtype)
    qall[me, 1] = qtmp[other].astype(qall.dtype)
    kvall[me, 0] = nk_ref[...]
    kvall[me, 1] = nv_ref[...]
    pl.semaphore_wait(barrier, depth - 1 + cell_size - 1 + requests * (groups - 1))

    def remote(src, dst, send_sem, recv_sem, **device):
        return pltpu.make_async_remote_copy(
            src_ref=src, dst_ref=dst, send_sem=send_sem, recv_sem=recv_sem, device_id=device, device_id_type=MESH
        )

    def landed(ref, sem):
        pltpu.make_async_copy(ref, ref, sem).wait()

    def by_distance(k):
        step = (k + 1) // 2
        return lax.rem(k, 2) * step + (1 - lax.rem(k, 2)) * (depth - step)

    def query_to(peer, source):
        return remote(qall.at[source], qall.at[source], z_send, z_recv.at[source // cell_size], ctx=peer)

    def send_query(k, c):
        query_to(lax.rem(me + cell_size * by_distance(depth - k), members), me).start()
        return c

    lax.fori_loop(1, depth, send_query, 0)

    def pass_on(source):
        where = q_recv.at[(source // near + side) % 2]
        for part, target in ((0, across), (1, diagonal), (1, partner)):
            remote(qall.at[source, part], qall.at[source, 0], q_send, where, ctx=target).start()

    pass_on(me)

    history_slab = pl.ds(history, history)
    give_k = remote(ck_ref.at[other], kbuf.at[history_slab], chip_send.at[0], chip_recv.at[0], ctx=partner)
    give_v = remote(cv_ref.at[other], vbuf.at[history_slab], chip_send.at[1], chip_recv.at[1], ctx=partner)
    give_w = remote(w_ref, wbuf.at[r], chip_send.at[2], chip_recv.at[2], ctx=partner)
    give_page = remote(kvall.at[me], kvall.at[me], chip_send.at[3], chip_recv.at[3], ctx=partner)
    give_page.start()
    give_k.start()
    give_v.start()

    def relay(k, c):
        source = lax.rem(me + cell_size * by_distance(k), members)
        query_to(me, source).wait_recv()
        pass_on(source)
        return c

    lax.fori_loop(1, depth, relay, 0)
    give_w.start()

    give_page.wait_recv()
    for source, target in ((0, kbuf), (1, vbuf)):
        ktail[...] = jnp.zeros_like(ktail)
        for j in range(2):
            ktail[pl.ds(j * page, page), :] = kvall[me - r + j, source, r].astype(jnp.float32)
        target[pl.ds(2 * history, tail), :] = ktail[...].astype(target.dtype)

    ones = jnp.ones((KEY_BLOCK, HD), jnp.bfloat16)
    row_token = lax.broadcasted_iota(jnp.int32, (rows, tail), 0) // heads
    tail_lane = lax.broadcasted_iota(jnp.int32, (rows, tail), 1)
    token_row = lax.broadcasted_iota(jnp.int32, (chunk, HD), 0)
    token_lane = lax.broadcasted_iota(jnp.int32, (chunk, HD), 1)
    lane = lax.broadcasted_iota(jnp.int32, (1, KEY_BLOCK), 1)

    def bias_of(device, offset):
        slot = lane + offset
        low = hist_ref[r] - device * half_size
        high = hist_ref[r] - (2 * members - 1 - device) * half_size + half_size
        return jnp.where(slot < jnp.where(slot < half_size, low, high), 0.0, FLOOR)

    dot_nt = functools.partial(
        lax.dot_general,
        dimension_numbers=(((1,), (1,)), ((), ())),
        preferred_element_type=jnp.float32,
    )

    steps = 2 * history // KEY_BLOCK
    relayed = qall.at[pl.ds(0, near - near // cell_size), 0]

    def attend(i, c):
        which = lax.rem(side + i, 2)
        first = which * near

        @pl.when(i == 0)
        def _():
            load_k.wait()

        landed(relayed, q_recv.at[i])
        queries = qall[pl.ds(first, near), 0].reshape(rows, HD)

        def score(b, peak):
            offset = pl.multiple_of(b * KEY_BLOCK, KEY_BLOCK)

            @pl.when((i == 0) & (offset == history))
            def _():
                give_k.wait_recv()

            given = offset // history
            block = dot_nt(queries, kbuf[pl.ds(offset, KEY_BLOCK), :])
            block = block + bias_of(me + (partner - me) * given, offset - history * given)
            scores[:, pl.ds(offset, KEY_BLOCK)] = block
            for p in range(KEY_BLOCK // HD):
                peak = jnp.maximum(peak, block[:, p * HD : (p + 1) * HD])
            return peak

        last = dot_nt(queries, kbuf[2 * history :, :])
        visible = (tail_lane < 2 * page) & (tail_lane + 2 * page * own <= row_token + which * chunk)
        last = jnp.where(visible, last, FLOOR)
        peak = jnp.max(lax.fori_loop(0, steps, score, last), axis=1, keepdims=True)
        weights = jnp.exp2((last - peak) * factor).astype(jnp.bfloat16)
        values = jnp.concatenate([vbuf[2 * history :, :], ones[:tail]], axis=1)
        acc[...] = jnp.dot(weights, values, preferred_element_type=jnp.float32)

        @pl.when(i == 0)
        def _():
            load_v.wait()
            give_v.wait_recv()

        def weigh(b, c):
            offset = pl.multiple_of(b * KEY_BLOCK, KEY_BLOCK)
            weights = jnp.exp2((scores[:, pl.ds(offset, KEY_BLOCK)] - peak) * factor).astype(jnp.bfloat16)
            values = jnp.concatenate([vbuf[pl.ds(offset, KEY_BLOCK), :], ones], axis=1)
            acc[...] += jnp.dot(weights, values, preferred_element_type=jnp.float32)
            return c

        lax.fori_loop(0, steps, weigh, 0)
        total = acc[:, HD:]
        lse[...] = peak * factor + jnp.log2(total)
        ready[...] = acc[:, :HD] / total

        base = (1 - which) * heads
        for h in range(heads):
            picked = pl.ds(h, chunk, stride=heads)
            osend[base + h] = ready[picked, :].astype(osend.dtype)
            lsend[base + h] = jnp.sum(jnp.where(token_row == token_lane, lse[picked, :], 0.0), axis=0, keepdims=True)

        def send_piece(k, c):
            target = base + lax.rem(k + own, heads)

            @pl.when(target != own)
            def _():
                remote(osend.at[target], orecv.at[own], o_send, o_recv, ctx=requests * target + r).start()
                remote(lsend.at[target], lrecv.at[own], l_send, l_recv, ctx=requests * target + r).start()

            return c

        lax.fori_loop(0, heads, send_piece, 0)
        return c

    lax.fori_loop(0, 2, attend, 0)

    def send_page(k, c):
        peer = lax.rem(me + k, members)

        @pl.when(peer != partner)
        def _():
            remote(kvall.at[me], kvall.at[me], page_send, page_recv, ctx=peer).start()

        return c

    lax.fori_loop(1, members, send_page, 0)

    orecv[own] = osend[own]
    lrecv[own] = lsend[own]
    landed(lrecv.at[pl.ds(0, owners - 1)], l_recv)
    levels = lrecv[...].reshape(owners, HD)
    levels = jnp.concatenate([levels, jnp.full((HD - owners, HD), FLOOR, jnp.float32)], axis=0)
    levels = levels.T[:chunk]
    share = jnp.exp2(levels - jnp.max(levels, axis=1, keepdims=True))
    share = share / jnp.sum(share, axis=1, keepdims=True)
    landed(orecv.at[pl.ds(0, owners - 1)], o_recv)
    done = jnp.zeros((chunk, HD), jnp.float32)
    for s in range(owners):
        done = done + share[:, s : s + 1] * orecv[s].astype(jnp.float32)
    place = abuf.at[lax.rem(own, heads), pl.ds(pl.multiple_of((1 - side) * chunk, chunk), chunk)]
    place[...] = done.astype(abuf.dtype)

    def send_finished(k, c):
        remote(place, place, f_send, f_recv, ctx=lax.rem(me + requests * k, members)).start()
        return c

    lax.fori_loop(1, owners, send_finished, 0)

    landed(kvall.at[pl.ds(0, members - 2)], page_recv)
    for s in range(requests):
        source = jnp.int32(0)
        for b in range(members):
            source = jnp.maximum(source, jnp.where(owner_ref[s, b] == me, b, 0))
        for kind in range(2):
            pages_ref[kind, s] = kvall[source, kind, s]
    load_w.wait()
    give_w.wait_recv()

    flat = abuf.reshape(owners, chunk, HD)
    landed(flat.at[pl.ds(0, owners - 1)], f_recv)
    rows_in = jnp.concatenate([abuf[h] for h in range(heads)], axis=1)
    for j in range(requests):
        part = jnp.dot(rows_in, wbuf[j], preferred_element_type=jnp.float32).astype(psend.dtype)
        for g in range(groups):
            psend[g, j] = part[g * share_rows : (g + 1) * share_rows]

    def send_part(k, c):
        peer = lax.rem(mine + k, groups)
        for j in range(requests):
            remote(psend.at[peer, j], precv.at[mine, r], p_send, p_recv, ctx=me - r + j, tp=peer).start()
        return c

    lax.fori_loop(1, groups, send_part, 0)
    remote(psend.at[mine, other], precv.at[mine, r], p_send, p_recv, ctx=partner).start()
    precv[mine, r] = psend[mine, r]
    flat_parts = precv.reshape(requests * groups, share_rows, precv.shape[3])
    landed(flat_parts.at[pl.ds(0, requests * groups - 1)], p_recv)
    full = precv[0].astype(jnp.float32)
    for g in range(1, groups):
        full = full + precv[g].astype(jnp.float32)
    out_ref[...] = full

    for give in (give_k, give_v, give_w, give_page):
        give.wait_send()
    landed(qall.at[pl.ds(0, depth - 1)], z_send)
    for _ in range(2):
        landed(relayed, q_send)
    landed(kvall.at[pl.ds(0, members - 2)], page_send)
    landed(orecv.at[pl.ds(0, owners - 1)], o_send)
    landed(lrecv.at[pl.ds(0, owners - 1)], l_send)
    landed(flat.at[pl.ds(0, owners - 1)], f_send)
    landed(flat_parts.at[pl.ds(0, requests * groups - 1)], p_send)


def finish(full_ref, pages_ref, attended_ref, keys_ref, values_ref):
    parts = [full_ref[r] for r in range(full_ref.shape[0])]
    attended_ref[...] = jnp.stack(parts, axis=1).astype(attended_ref.dtype)
    keys_ref[0] = pages_ref[0]
    values_ref[0] = pages_ref[1]


def on_device(queries, new_keys, new_values, cache_keys, cache_values, hist_len, page_owner, out_weight):
    members = lax.axis_size("ctx")
    groups = lax.axis_size("tp")
    page, requests, width = queries.shape
    history = cache_keys.shape[1]
    heads = width // HD
    turn = page * members
    chunk = turn // 2
    owners = members // requests
    share_rows = turn // groups
    columns = out_weight.shape[1]
    vmem = pl.BlockSpec(memory_space=pltpu.VMEM)
    smem = pl.BlockSpec(memory_space=pltpu.SMEM)
    anywhere = pl.BlockSpec(memory_space=pl.ANY)
    bf16, f32 = jnp.bfloat16, jnp.float32
    dma = pltpu.SemaphoreType.DMA
    full, pages = pl.pallas_call(
        functools.partial(kernel, members, groups),
        out_shape=(
            jax.ShapeDtypeStruct((requests, share_rows, columns), f32),
            jax.ShapeDtypeStruct((2, *new_keys.shape), bf16),
        ),
        in_specs=[vmem, vmem, vmem, anywhere, anywhere, smem, smem, anywhere],
        out_specs=[vmem, vmem],
        scratch_shapes=[
            pltpu.VMEM((2 * history + HD, HD), bf16),
            pltpu.VMEM((2 * history + HD, HD), bf16),
            pltpu.VMEM((requests, *out_weight.shape), bf16),
            pltpu.VMEM((requests, page * heads, HD), f32),
            pltpu.VMEM((HD, HD), f32),
            pltpu.VMEM((members, requests, page * heads, HD), bf16),
            pltpu.VMEM((members, 2, *new_keys.shape), bf16),
            pltpu.VMEM((chunk * heads, 2 * history), f32),
            pltpu.VMEM((chunk * heads, 2 * HD), f32),
            pltpu.VMEM((chunk * heads, HD), f32),
            pltpu.VMEM((chunk * heads, HD), f32),
            pltpu.VMEM((owners, chunk, HD), bf16),
            pltpu.VMEM((owners, 1, HD), f32),
            pltpu.VMEM((owners, chunk, HD), bf16),
            pltpu.VMEM((owners, 1, HD), f32),
            pltpu.VMEM((heads, turn, HD), bf16),
            pltpu.VMEM((groups, requests, share_rows, columns), bf16),
            pltpu.VMEM((groups, requests, share_rows, columns), bf16),
            dma((3,)),
            dma((4,)),
            dma((4,)),
            dma(()),
            dma((members // 4,)),
            dma(()),
            dma((2,)),
            dma(()),
            dma(()),
            dma(()),
            dma(()),
            dma(()),
            dma(()),
            dma(()),
            dma(()),
            dma(()),
            dma(()),
        ],
        compiler_params=pltpu.CompilerParams(collective_id=0, has_side_effects=True),
    )(queries, new_keys, new_values, cache_keys, cache_values, hist_len, page_owner, out_weight)
    pages_shape = jax.ShapeDtypeStruct((1, *new_keys.shape), bf16)
    return pl.pallas_call(
        finish,
        out_shape=(jax.ShapeDtypeStruct((share_rows, requests, columns), bf16), pages_shape, pages_shape),
        in_specs=[vmem, vmem],
        out_specs=[vmem, vmem, vmem],
    )(full, pages)


def solution(mesh):
    return jax.shard_map(
        on_device,
        mesh=mesh,
        in_specs=(
            P("ctx", None, "tp"),
            P(None, "ctx", "tp"),
            P(None, "ctx", "tp"),
            P(None, "ctx", "tp"),
            P(None, "ctx", "tp"),
            P(),
            P(),
            P("tp", "ctx"),
        ),
        out_specs=(P("tp", None, "ctx"), P("ctx", None, None, "tp"), P("ctx", None, None, "tp")),
        check_vma=False,
    )
```

```python
import functools
import math

import jax
import jax.numpy as jnp
from jax import lax
from jax.experimental import pallas as pl
from jax.experimental.pallas import tpu as pltpu
from jax.sharding import PartitionSpec as P

HD = 128
FLOOR = -1e30
KEY_BLOCK = 4096
MESH = pl.DeviceIdType.MESH


def kernel(
    members,
    groups,
    q_ref,
    nk_ref,
    nv_ref,
    ck_ref,
    cv_ref,
    hist_ref,
    owner_ref,
    w_ref,
    out_ref,
    pages_ref,
    kbuf,
    vbuf,
    wbuf,
    qtmp,
    ktail,
    qall,
    kvall,
    scores,
    acc,
    ready,
    lse,
    osend,
    lsend,
    orecv,
    lrecv,
    abuf,
    psend,
    precv,
    load_sem,
    chip_send,
    chip_recv,
    z_send,
    z_recv,
    q_send,
    q_recv,
    page_send,
    page_recv,
    o_send,
    o_recv,
    l_send,
    l_recv,
    f_send,
    f_recv,
    p_send,
    p_recv,
):
    me = lax.axis_index("ctx")
    mine = lax.axis_index("tp")
    requests, history = ck_ref.shape[:2]
    page = q_ref.shape[0]
    heads = q_ref.shape[2] // HD
    turn = page * members
    chunk = turn // 2
    rows = chunk * heads
    half_size = history // 2
    owners = members // requests
    near = members // 2
    quarter = turn // groups // 2
    share_rows = turn // groups
    tail = kbuf.shape[0] - 2 * history
    factor = math.log2(math.e) / math.sqrt(HD)

    r = lax.rem(me, 2)
    other = 1 - r
    partner = me + 1 - 2 * r
    cell_size = 4
    depth = members // cell_size
    across = me + 2 - 4 * lax.rem(me // 2, 2)
    diagonal = across + 1 - 2 * r
    own = me // 2
    side = lax.rem(own, 2)
    level = own // 2

    load_k = pltpu.make_async_copy(ck_ref.at[r], kbuf.at[pl.ds(0, history)], load_sem.at[0])
    load_v = pltpu.make_async_copy(cv_ref.at[r], vbuf.at[pl.ds(0, history)], load_sem.at[1])
    load_w = pltpu.make_async_copy(w_ref, wbuf.at[r], load_sem.at[2])
    load_k.start()
    load_v.start()
    load_w.start()

    barrier = pltpu.get_barrier_semaphore()

    def greet(**device):
        pl.semaphore_signal(barrier, inc=1, device_id=device, device_id_type=MESH)

    def greet_z(k, c):
        greet(ctx=lax.rem(me + cell_size * k, members))
        return c

    def greet_tp(k, c):
        for j in range(requests):
            greet(ctx=me - r + j, tp=lax.rem(mine + k, groups))
        return c

    lax.fori_loop(1, depth, greet_z, 0)
    for cell in (partner, across, diagonal):
        greet(ctx=cell)
    lax.fori_loop(1, groups, greet_tp, 0)

    for t in range(page):
        row = q_ref[t].astype(jnp.float32)
        for h in range(heads):
            for s in range(requests):
                qtmp[s, pl.ds(t * heads + h, 1), :] = row[s : s + 1, h * HD : (h + 1) * HD]
    def slot_of(device):
        return lax.rem(device // 2, 2) * near + device // 4 * 2 + lax.rem(device, 2)

    qall[slot_of(me), 0] = qtmp[r].astype(qall.dtype)
    qall[slot_of(me), 1] = qtmp[other].astype(qall.dtype)
    kvall[me, 0] = nk_ref[...]
    kvall[me, 1] = nv_ref[...]
    pl.semaphore_wait(barrier, depth - 1 + cell_size - 1 + requests * (groups - 1))

    def remote(src, dst, send_sem, recv_sem, **device):
        return pltpu.make_async_remote_copy(
            src_ref=src, dst_ref=dst, send_sem=send_sem, recv_sem=recv_sem, device_id=device, device_id_type=MESH
        )

    def landed(ref, sem):
        pltpu.make_async_copy(ref, ref, sem).wait()

    def by_distance(k):
        step = (k + 1) // 2
        return lax.rem(k, 2) * step + (1 - lax.rem(k, 2)) * (depth - step)

    def query_to(peer, source):
        block = qall.at[slot_of(source)]
        return remote(block, block, z_send, z_recv.at[source // cell_size], ctx=peer)

    def send_query(k, c):
        query_to(lax.rem(me + cell_size * by_distance(depth - k), members), me).start()
        return c

    lax.fori_loop(1, depth, send_query, 0)

    def pass_on(source):
        slot = slot_of(source)
        for part, target, chunk_id in ((0, across, 1), (1, diagonal, 1), (1, partner, 0)):
            remote(qall.at[slot, part], qall.at[slot, 0], q_send, q_recv.at[chunk_id], ctx=target).start()

    pass_on(me)

    history_slab = pl.ds(history, history)
    give_k = remote(ck_ref.at[other], kbuf.at[history_slab], chip_send.at[0], chip_recv.at[0], ctx=partner)
    give_v = remote(cv_ref.at[other], vbuf.at[history_slab], chip_send.at[1], chip_recv.at[1], ctx=partner)
    give_w = remote(w_ref, wbuf.at[r], chip_send.at[2], chip_recv.at[2], ctx=partner)
    give_page = remote(kvall.at[me], kvall.at[me], chip_send.at[3], chip_recv.at[3], ctx=partner)
    give_page.start()
    give_k.start()
    give_v.start()

    def relay(k, c):
        source = lax.rem(me + cell_size * by_distance(k), members)
        query_to(me, source).wait_recv()
        pass_on(source)
        return c

    lax.fori_loop(1, depth, relay, 0)
    give_w.start()

    give_page.wait_recv()
    for source, target in ((0, kbuf), (1, vbuf)):
        ktail[...] = jnp.zeros_like(ktail)
        for j in range(2):
            ktail[pl.ds(j * page, page), :] = kvall[me - r + j, source, r].astype(jnp.float32)
        target[pl.ds(2 * history, tail), :] = ktail[...].astype(target.dtype)

    ones = jnp.ones((KEY_BLOCK, HD), jnp.bfloat16)
    row_index = lax.broadcasted_iota(jnp.int32, (rows, tail), 0) // heads
    row_token = row_index // quarter * (2 * quarter) + lax.rem(row_index, quarter)
    tail_lane = lax.broadcasted_iota(jnp.int32, (rows, tail), 1)
    token_row = lax.broadcasted_iota(jnp.int32, (chunk, HD), 0)
    token_lane = lax.broadcasted_iota(jnp.int32, (chunk, HD), 1)
    lane = lax.broadcasted_iota(jnp.int32, (1, KEY_BLOCK), 1)

    def bias_of(device, offset):
        slot = lane + offset
        low = hist_ref[r] - device * half_size
        high = hist_ref[r] - (2 * members - 1 - device) * half_size + half_size
        return jnp.where(slot < jnp.where(slot < half_size, low, high), 0.0, FLOOR)

    dot_nt = functools.partial(
        lax.dot_general,
        dimension_numbers=(((1,), (1,)), ((), ())),
        preferred_element_type=jnp.float32,
    )

    steps = 2 * history // KEY_BLOCK

    def attend(i, c):
        which = lax.rem(side + i, 2)
        first = which * near

        @pl.when(i == 0)
        def _():
            load_k.wait()
            landed(qall.at[pl.ds(0, depth), 0], q_recv.at[0])

        @pl.when(i == 1)
        def _():
            landed(qall.at[pl.ds(0, near), 0], q_recv.at[1])

        queries = qall[pl.ds(first, near), 0].reshape(rows, HD)

        def score(b, peak):
            offset = pl.multiple_of(b * KEY_BLOCK, KEY_BLOCK)

            @pl.when((i == 0) & (offset == history))
            def _():
                give_k.wait_recv()

            given = offset // history
            block = dot_nt(queries, kbuf[pl.ds(offset, KEY_BLOCK), :])
            block = block + bias_of(me + (partner - me) * given, offset - history * given)
            scores[:, pl.ds(offset, KEY_BLOCK)] = block
            for p in range(KEY_BLOCK // HD):
                peak = jnp.maximum(peak, block[:, p * HD : (p + 1) * HD])
            return peak

        last = dot_nt(queries, kbuf[2 * history :, :])
        visible = (tail_lane < 2 * page) & (tail_lane + 2 * page * own <= row_token + which * quarter)
        last = jnp.where(visible, last, FLOOR)
        peak = jnp.max(lax.fori_loop(0, steps, score, last), axis=1, keepdims=True)
        weights = jnp.exp2((last - peak) * factor).astype(jnp.bfloat16)
        values = jnp.concatenate([vbuf[2 * history :, :], ones[:tail]], axis=1)
        acc[...] = jnp.dot(weights, values, preferred_element_type=jnp.float32)

        @pl.when(i == 0)
        def _():
            load_v.wait()
            give_v.wait_recv()

        def weigh(b, c):
            offset = pl.multiple_of(b * KEY_BLOCK, KEY_BLOCK)
            weights = jnp.exp2((scores[:, pl.ds(offset, KEY_BLOCK)] - peak) * factor).astype(jnp.bfloat16)
            values = jnp.concatenate([vbuf[pl.ds(offset, KEY_BLOCK), :], ones], axis=1)
            acc[...] += jnp.dot(weights, values, preferred_element_type=jnp.float32)
            return c

        lax.fori_loop(0, steps, weigh, 0)
        total = acc[:, HD:]
        lse[...] = peak * factor + jnp.log2(total)
        ready[...] = acc[:, :HD] / total

        for h in range(heads):
            picked = pl.ds(h, chunk, stride=heads)
            osend[2 * h + 1 - which] = ready[picked, :].astype(osend.dtype)
            lsend[2 * h + 1 - which] = jnp.sum(jnp.where(token_row == token_lane, lse[picked, :], 0.0), axis=0, keepdims=True)

        def send_piece(k, c):
            target = 2 * lax.rem(k + level, heads) + 1 - which

            @pl.when(target != own)
            def _():
                remote(osend.at[target], orecv.at[own], o_send, o_recv, ctx=requests * target + r).start()
                remote(lsend.at[target], lrecv.at[own], l_send, l_recv, ctx=requests * target + r).start()

            return c

        lax.fori_loop(0, heads, send_piece, 0)
        return c

    lax.fori_loop(0, 2, attend, 0)

    def send_page(k, c):
        peer = lax.rem(me + k, members)

        @pl.when(peer != partner)
        def _():
            remote(kvall.at[me], kvall.at[me], page_send, page_recv, ctx=peer).start()

        return c

    lax.fori_loop(1, members, send_page, 0)

    orecv[own] = osend[own]
    lrecv[own] = lsend[own]
    landed(lrecv.at[pl.ds(0, owners - 1)], l_recv)
    levels = lrecv[...].reshape(owners, HD)
    levels = jnp.concatenate([levels, jnp.full((HD - owners, HD), FLOOR, jnp.float32)], axis=0)
    levels = levels.T[:chunk]
    share = jnp.exp2(levels - jnp.max(levels, axis=1, keepdims=True))
    share = share / jnp.sum(share, axis=1, keepdims=True)
    landed(orecv.at[pl.ds(0, owners - 1)], o_recv)
    done = jnp.zeros((chunk, HD), jnp.float32)
    for s in range(owners):
        done = done + share[:, s : s + 1] * orecv[s].astype(jnp.float32)
    place = abuf.at[level, pl.ds(pl.multiple_of((1 - side) * chunk, chunk), chunk)]
    place[...] = done.astype(abuf.dtype)

    def send_finished(k, c):
        remote(place, place, f_send, f_recv, ctx=lax.rem(me + requests * k, members)).start()
        return c

    lax.fori_loop(1, owners, send_finished, 0)

    landed(kvall.at[pl.ds(0, members - 2)], page_recv)
    for s in range(requests):
        source = jnp.int32(0)
        for b in range(members):
            source = jnp.maximum(source, jnp.where(owner_ref[s, b] == me, b, 0))
        for kind in range(2):
            pages_ref[kind, s] = kvall[source, kind, s]
    load_w.wait()
    give_w.wait_recv()

    flat = abuf.reshape(owners, chunk, HD)
    landed(flat.at[pl.ds(0, owners - 1)], f_recv)
    rows_in = jnp.concatenate([abuf[h] for h in range(heads)], axis=1)
    for j in range(requests):
        part = jnp.dot(rows_in, wbuf[j], preferred_element_type=jnp.float32)
        for g in range(groups):
            halves = [part[y * chunk + g * quarter : y * chunk + (g + 1) * quarter] for y in range(2)]
            psend[g, j] = jnp.concatenate(halves, axis=0).astype(psend.dtype)

    def send_part(k, c):
        peer = lax.rem(mine + k, groups)
        for j in range(requests):
            remote(psend.at[peer, j], precv.at[mine, r], p_send, p_recv, ctx=me - r + j, tp=peer).start()
        return c

    lax.fori_loop(1, groups, send_part, 0)
    remote(psend.at[mine, other], precv.at[mine, r], p_send, p_recv, ctx=partner).start()
    precv[mine, r] = psend[mine, r]
    flat_parts = precv.reshape(requests * groups, share_rows, precv.shape[3])
    landed(flat_parts.at[pl.ds(0, requests * groups - 1)], p_recv)
    full = precv[0].astype(jnp.float32)
    for g in range(1, groups):
        full = full + precv[g].astype(jnp.float32)
    out_ref[...] = full

    for give in (give_k, give_v, give_w, give_page):
        give.wait_send()
    landed(qall.at[pl.ds(0, depth - 1)], z_send)
    landed(qall.at[pl.ds(0, 3 * depth), 0], q_send)
    landed(kvall.at[pl.ds(0, members - 2)], page_send)
    landed(orecv.at[pl.ds(0, owners - 1)], o_send)
    landed(lrecv.at[pl.ds(0, owners - 1)], l_send)
    landed(flat.at[pl.ds(0, owners - 1)], f_send)
    landed(flat_parts.at[pl.ds(0, requests * groups - 1)], p_send)


def finish(full_ref, pages_ref, attended_ref, keys_ref, values_ref):
    parts = [full_ref[r] for r in range(full_ref.shape[0])]
    attended_ref[...] = jnp.stack(parts, axis=1).astype(attended_ref.dtype)
    keys_ref[0] = pages_ref[0]
    values_ref[0] = pages_ref[1]


def on_device(queries, new_keys, new_values, cache_keys, cache_values, hist_len, page_owner, out_weight):
    members = lax.axis_size("ctx")
    groups = lax.axis_size("tp")
    page, requests, width = queries.shape
    history = cache_keys.shape[1]
    heads = width // HD
    turn = page * members
    chunk = turn // 2
    owners = members // requests
    share_rows = turn // groups
    columns = out_weight.shape[1]
    vmem = pl.BlockSpec(memory_space=pltpu.VMEM)
    smem = pl.BlockSpec(memory_space=pltpu.SMEM)
    anywhere = pl.BlockSpec(memory_space=pl.ANY)
    bf16, f32 = jnp.bfloat16, jnp.float32
    dma = pltpu.SemaphoreType.DMA
    full, pages = pl.pallas_call(
        functools.partial(kernel, members, groups),
        out_shape=(
            jax.ShapeDtypeStruct((requests, share_rows, columns), f32),
            jax.ShapeDtypeStruct((2, *new_keys.shape), bf16),
        ),
        in_specs=[vmem, vmem, vmem, anywhere, anywhere, smem, smem, anywhere],
        out_specs=[vmem, vmem],
        scratch_shapes=[
            pltpu.VMEM((2 * history + HD, HD), bf16),
            pltpu.VMEM((2 * history + HD, HD), bf16),
            pltpu.VMEM((requests, *out_weight.shape), bf16),
            pltpu.VMEM((requests, page * heads, HD), f32),
            pltpu.VMEM((HD, HD), f32),
            pltpu.VMEM((members, requests, page * heads, HD), bf16),
            pltpu.VMEM((members, 2, *new_keys.shape), bf16),
            pltpu.VMEM((chunk * heads, 2 * history), f32),
            pltpu.VMEM((chunk * heads, 2 * HD), f32),
            pltpu.VMEM((chunk * heads, HD), f32),
            pltpu.VMEM((chunk * heads, HD), f32),
            pltpu.VMEM((owners, chunk, HD), bf16),
            pltpu.VMEM((owners, 1, HD), f32),
            pltpu.VMEM((owners, chunk, HD), bf16),
            pltpu.VMEM((owners, 1, HD), f32),
            pltpu.VMEM((heads, turn, HD), bf16),
            pltpu.VMEM((groups, requests, share_rows, columns), bf16),
            pltpu.VMEM((groups, requests, share_rows, columns), bf16),
            dma((3,)),
            dma((4,)),
            dma((4,)),
            dma(()),
            dma((members // 4,)),
            dma(()),
            dma((2,)),
            dma(()),
            dma(()),
            dma(()),
            dma(()),
            dma(()),
            dma(()),
            dma(()),
            dma(()),
            dma(()),
            dma(()),
        ],
        compiler_params=pltpu.CompilerParams(collective_id=0, has_side_effects=True),
    )(queries, new_keys, new_values, cache_keys, cache_values, hist_len, page_owner, out_weight)
    pages_shape = jax.ShapeDtypeStruct((1, *new_keys.shape), bf16)
    return pl.pallas_call(
        finish,
        out_shape=(jax.ShapeDtypeStruct((share_rows, requests, columns), bf16), pages_shape, pages_shape),
        in_specs=[vmem, vmem],
        out_specs=[vmem, vmem, vmem],
    )(full, pages)


def solution(mesh):
    return jax.shard_map(
        on_device,
        mesh=mesh,
        in_specs=(
            P("ctx", None, "tp"),
            P(None, "ctx", "tp"),
            P(None, "ctx", "tp"),
            P(None, "ctx", "tp"),
            P(None, "ctx", "tp"),
            P(),
            P(),
            P("tp", "ctx"),
        ),
        out_specs=(P("tp", None, "ctx"), P("ctx", None, None, "tp"), P("ctx", None, None, "tp")),
        check_vma=False,
    )
```

```python
import functools
import math

import jax
import jax.numpy as jnp
from jax import lax
from jax.experimental import pallas as pl
from jax.experimental.pallas import tpu as pltpu
from jax.sharding import PartitionSpec as P

HD = 128
FLOOR = -1e30
KEY_BLOCK = 4096
MESH = pl.DeviceIdType.MESH


def kernel(
    members,
    groups,
    q_hbm,
    nk_hbm,
    nv_hbm,
    ck_ref,
    cv_ref,
    hist_hbm,
    owner_hbm,
    w_ref,
    out_ref,
    pages_ref,
    q_ref,
    hist_ref,
    owner_ref,
    kbuf,
    vbuf,
    wbuf,
    qtmp,
    ktail,
    qall,
    kvall,
    scores,
    acc,
    ready,
    lse,
    osend,
    lsend,
    orecv,
    lrecv,
    abuf,
    psend,
    precv,
    load_sem,
    chip_send,
    chip_recv,
    z_send,
    z_recv,
    q_send,
    q_recv,
    page_send,
    page_recv,
    o_send,
    o_recv,
    l_send,
    l_recv,
    f_send,
    f_recv,
    p_send,
    p_recv,
):
    me = lax.axis_index("ctx")
    mine = lax.axis_index("tp")
    requests, history = ck_ref.shape[:2]
    page = q_hbm.shape[0]
    heads = q_hbm.shape[2] // HD
    turn = page * members
    chunk = turn // 2
    rows = chunk * heads
    half_size = history // 2
    owners = members // requests
    near = members // 2
    quarter = turn // groups // 2
    share_rows = turn // groups
    tail = kbuf.shape[0] - 2 * history
    factor = math.log2(math.e) / math.sqrt(HD)

    r = lax.rem(me, 2)
    other = 1 - r
    partner = me + 1 - 2 * r
    cell_size = 4
    depth = members // cell_size
    across = me + 2 - 4 * lax.rem(me // 2, 2)
    diagonal = across + 1 - 2 * r
    own = me // 2
    side = lax.rem(own, 2)
    level = own // 2

    load_k = pltpu.make_async_copy(ck_ref.at[r], kbuf.at[pl.ds(0, history)], load_sem.at[0])
    load_v = pltpu.make_async_copy(cv_ref.at[r], vbuf.at[pl.ds(0, history)], load_sem.at[1])
    load_w = pltpu.make_async_copy(w_ref, wbuf.at[r], load_sem.at[2])
    load_q = pltpu.make_async_copy(q_hbm, q_ref, load_sem.at[3])
    load_pages = (
        pltpu.make_async_copy(nk_hbm, kvall.at[me, 0], load_sem.at[4]),
        pltpu.make_async_copy(nv_hbm, kvall.at[me, 1], load_sem.at[5]),
    )
    load_hist = pltpu.make_async_copy(hist_hbm, hist_ref, load_sem.at[6])
    load_owner = pltpu.make_async_copy(owner_hbm, owner_ref, load_sem.at[7])
    load_q.start()

    barrier = pltpu.get_barrier_semaphore()

    def greet(**device):
        pl.semaphore_signal(barrier, inc=1, device_id=device, device_id_type=MESH)

    def by_distance(k):
        step = (k + 1) // 2
        return lax.rem(k, 2) * step + (1 - lax.rem(k, 2)) * (depth - step)

    def greet_z(k, c):
        greet(ctx=lax.rem(me + cell_size * by_distance(depth - k), members))
        return c

    def greet_tp(k, c):
        for j in range(requests):
            greet(ctx=me - r + j, tp=lax.rem(mine + k, groups))
        return c

    lax.fori_loop(1, depth, greet_z, 0)
    for cell in (partner, across, diagonal):
        greet(ctx=cell)
    lax.fori_loop(1, groups, greet_tp, 0)
    for copy in (*load_pages, load_hist, load_owner, load_k, load_v, load_w):
        copy.start()
    load_q.wait()

    for t in range(page):
        row = q_ref[t].astype(jnp.float32)
        for h in range(heads):
            for s in range(requests):
                qtmp[s, pl.ds(t * heads + h, 1), :] = row[s : s + 1, h * HD : (h + 1) * HD]
    def slot_of(device):
        return lax.rem(device // 2, 2) * near + device // 4 * 2 + lax.rem(device, 2)

    qall[slot_of(me), 0] = qtmp[r].astype(qall.dtype)
    qall[slot_of(me), 1] = qtmp[other].astype(qall.dtype)
    pl.semaphore_wait(barrier, depth - 1 + cell_size - 1 + requests * (groups - 1))

    def remote(src, dst, send_sem, recv_sem, **device):
        return pltpu.make_async_remote_copy(
            src_ref=src, dst_ref=dst, send_sem=send_sem, recv_sem=recv_sem, device_id=device, device_id_type=MESH
        )

    def landed(ref, sem):
        pltpu.make_async_copy(ref, ref, sem).wait()

    def query_to(peer, source):
        block = qall.at[slot_of(source)]
        return remote(block, block, z_send, z_recv.at[source // cell_size], ctx=peer)

    def send_query(k, c):
        query_to(lax.rem(me + cell_size * by_distance(depth - k), members), me).start()
        return c

    lax.fori_loop(1, depth, send_query, 0)

    def pass_on(source):
        slot = slot_of(source)
        for part, target, chunk_id in ((0, across, 1), (1, diagonal, 1), (1, partner, 0)):
            remote(qall.at[slot, part], qall.at[slot, 0], q_send, q_recv.at[chunk_id], ctx=target).start()

    pass_on(me)

    history_slab = pl.ds(history, history)
    give_k = remote(ck_ref.at[other], kbuf.at[history_slab], chip_send.at[0], chip_recv.at[0], ctx=partner)
    give_v = remote(cv_ref.at[other], vbuf.at[history_slab], chip_send.at[1], chip_recv.at[1], ctx=partner)
    give_w = remote(w_ref, wbuf.at[r], chip_send.at[2], chip_recv.at[2], ctx=partner)
    give_page = remote(kvall.at[me], kvall.at[me], chip_send.at[3], chip_recv.at[3], ctx=partner)
    for copy in load_pages:
        copy.wait()
    give_page.start()
    give_k.start()
    give_v.start()

    def relay(k, c):
        source = lax.rem(me + cell_size * by_distance(k), members)
        query_to(me, source).wait_recv()
        pass_on(source)
        return c

    lax.fori_loop(1, depth, relay, 0)
    give_w.start()

    give_page.wait_recv()
    for source, target in ((0, kbuf), (1, vbuf)):
        ktail[...] = jnp.zeros_like(ktail)
        for j in range(2):
            ktail[pl.ds(j * page, page), :] = kvall[me - r + j, source, r].astype(jnp.float32)
        target[pl.ds(2 * history, tail), :] = ktail[...].astype(target.dtype)

    ones = jnp.ones((KEY_BLOCK, HD), jnp.bfloat16)
    row_index = lax.broadcasted_iota(jnp.int32, (rows, tail), 0) // heads
    row_token = row_index // quarter * (2 * quarter) + lax.rem(row_index, quarter)
    tail_lane = lax.broadcasted_iota(jnp.int32, (rows, tail), 1)
    token_row = lax.broadcasted_iota(jnp.int32, (chunk, HD), 0)
    token_lane = lax.broadcasted_iota(jnp.int32, (chunk, HD), 1)
    lane = lax.broadcasted_iota(jnp.int32, (1, KEY_BLOCK), 1)

    def bias_of(device, offset):
        slot = lane + offset
        low = hist_ref[r] - device * half_size
        high = hist_ref[r] - (2 * members - 1 - device) * half_size + half_size
        return jnp.where(slot < jnp.where(slot < half_size, low, high), 0.0, FLOOR)

    dot_nt = functools.partial(
        lax.dot_general,
        dimension_numbers=(((1,), (1,)), ((), ())),
        preferred_element_type=jnp.float32,
    )

    steps = 2 * history // KEY_BLOCK

    def attend(i, c):
        which = lax.rem(side + i, 2)
        first = which * near

        @pl.when(i == 0)
        def _():
            load_k.wait()
            landed(qall.at[pl.ds(0, depth), 0], q_recv.at[0])

        @pl.when(i == 1)
        def _():
            landed(qall.at[pl.ds(0, near), 0], q_recv.at[1])

        queries = qall[pl.ds(first, near), 0].reshape(rows, HD)

        def score(b, peak):
            offset = pl.multiple_of(b * KEY_BLOCK, KEY_BLOCK)

            @pl.when((i == 0) & (offset == history))
            def _():
                give_k.wait_recv()

            given = offset // history
            block = dot_nt(queries, kbuf[pl.ds(offset, KEY_BLOCK), :])
            block = block + bias_of(me + (partner - me) * given, offset - history * given)
            scores[:, pl.ds(offset, KEY_BLOCK)] = block
            for p in range(KEY_BLOCK // HD):
                peak = jnp.maximum(peak, block[:, p * HD : (p + 1) * HD])
            return peak

        last = dot_nt(queries, kbuf[2 * history :, :])
        visible = (tail_lane < 2 * page) & (tail_lane + 2 * page * own <= row_token + which * quarter)
        last = jnp.where(visible, last, FLOOR)
        peak = jnp.max(lax.fori_loop(0, steps, score, last), axis=1, keepdims=True)
        weights = jnp.exp2((last - peak) * factor).astype(jnp.bfloat16)
        values = jnp.concatenate([vbuf[2 * history :, :], ones[:tail]], axis=1)
        acc[...] = jnp.dot(weights, values, preferred_element_type=jnp.float32)

        @pl.when(i == 0)
        def _():
            load_v.wait()
            give_v.wait_recv()

        def weigh(b, c):
            offset = pl.multiple_of(b * KEY_BLOCK, KEY_BLOCK)
            weights = jnp.exp2((scores[:, pl.ds(offset, KEY_BLOCK)] - peak) * factor).astype(jnp.bfloat16)
            values = jnp.concatenate([vbuf[pl.ds(offset, KEY_BLOCK), :], ones], axis=1)
            acc[...] += jnp.dot(weights, values, preferred_element_type=jnp.float32)
            return c

        lax.fori_loop(0, steps, weigh, 0)
        total = acc[:, HD:]
        lse[...] = peak * factor + jnp.log2(total)
        ready[...] = acc[:, :HD] / total

        def pack(h):
            picked = pl.ds(h, chunk, stride=heads)
            target = 2 * h + 1 - which
            osend[target] = ready[picked, :].astype(osend.dtype)
            lsend[target] = jnp.sum(jnp.where(token_row == token_lane, lse[picked, :], 0.0), axis=0, keepdims=True)

        def send_piece(h):
            target = 2 * h + 1 - which

            @pl.when(target != own)
            def _():
                remote(osend.at[target], orecv.at[own], o_send, o_recv, ctx=requests * target + r).start()
                remote(lsend.at[target], lrecv.at[own], l_send, l_recv, ctx=requests * target + r).start()

        def turned(k):
            return lax.rem(k + level, heads)

        def piece(k, c):
            pack(turned(k))
            send_piece(turned(k - 1))
            return c

        pack(turned(0))
        lax.fori_loop(1, heads, piece, 0)
        send_piece(turned(heads - 1))
        return c

    load_hist.wait()
    load_owner.wait()
    lax.fori_loop(0, 2, attend, 0)

    def send_page(k, c):
        peer = lax.rem(me + k, members)

        @pl.when(peer != partner)
        def _():
            remote(kvall.at[me], kvall.at[me], page_send, page_recv, ctx=peer).start()

        return c

    lax.fori_loop(1, members, send_page, 0)

    orecv[own] = osend[own]
    lrecv[own] = lsend[own]
    landed(lrecv.at[pl.ds(0, owners - 1)], l_recv)
    levels = lrecv[...].reshape(owners, HD)
    levels = jnp.concatenate([levels, jnp.full((HD - owners, HD), FLOOR, jnp.float32)], axis=0)
    levels = levels.T[:chunk]
    share = jnp.exp2(levels - jnp.max(levels, axis=1, keepdims=True))
    share = share / jnp.sum(share, axis=1, keepdims=True)
    landed(orecv.at[pl.ds(0, owners - 1)], o_recv)
    done = jnp.zeros((chunk, HD), jnp.float32)
    for s in range(owners):
        done = done + share[:, s : s + 1] * orecv[s].astype(jnp.float32)
    place = abuf.at[level, pl.ds(pl.multiple_of((1 - side) * chunk, chunk), chunk)]
    place[...] = done.astype(abuf.dtype)

    def send_finished(k, c):
        remote(place, place, f_send, f_recv, ctx=lax.rem(me + requests * k, members)).start()
        return c

    lax.fori_loop(1, owners, send_finished, 0)

    landed(kvall.at[pl.ds(0, members - 2)], page_recv)
    for s in range(requests):
        source = jnp.int32(0)
        for b in range(members):
            source = jnp.maximum(source, jnp.where(owner_ref[s, b] == me, b, 0))
        for kind in range(2):
            pages_ref[kind, s] = kvall[source, kind, s]
    load_w.wait()
    give_w.wait_recv()

    flat = abuf.reshape(owners, chunk, HD)
    landed(flat.at[pl.ds(0, owners - 1)], f_recv)
    rows_in = jnp.concatenate([abuf[h] for h in range(heads)], axis=1)
    def project(j, c):
        part = jnp.dot(rows_in, wbuf[j], preferred_element_type=jnp.float32)
        for g in range(groups):
            halves = [part[y * chunk + g * quarter : y * chunk + (g + 1) * quarter] for y in range(2)]
            psend[g, j] = jnp.concatenate(halves, axis=0).astype(psend.dtype)
        return c

    lax.fori_loop(0, requests, project, 0)

    def send_part(k, c):
        peer = lax.rem(mine + k, groups)
        for j in range(requests):
            remote(psend.at[peer, j], precv.at[mine, r], p_send, p_recv, ctx=me - r + j, tp=peer).start()
        return c

    lax.fori_loop(1, groups, send_part, 0)
    remote(psend.at[mine, other], precv.at[mine, r], p_send, p_recv, ctx=partner).start()
    precv[mine, r] = psend[mine, r]
    flat_parts = precv.reshape(requests * groups, share_rows, precv.shape[3])
    landed(flat_parts.at[pl.ds(0, requests * groups - 1)], p_recv)
    full = precv[0].astype(jnp.float32)
    for g in range(1, groups):
        full = full + precv[g].astype(jnp.float32)
    out_ref[...] = full

    for give in (give_k, give_v, give_w, give_page):
        give.wait_send()
    landed(qall.at[pl.ds(0, depth - 1)], z_send)
    landed(qall.at[pl.ds(0, 3 * depth), 0], q_send)
    landed(kvall.at[pl.ds(0, members - 2)], page_send)
    landed(orecv.at[pl.ds(0, owners - 1)], o_send)
    landed(lrecv.at[pl.ds(0, owners - 1)], l_send)
    landed(flat.at[pl.ds(0, owners - 1)], f_send)
    landed(flat_parts.at[pl.ds(0, requests * groups - 1)], p_send)


def finish(full_ref, pages_ref, attended_ref, keys_ref, values_ref):
    parts = [full_ref[r] for r in range(full_ref.shape[0])]
    attended_ref[...] = jnp.stack(parts, axis=1).astype(attended_ref.dtype)
    keys_ref[0] = pages_ref[0]
    values_ref[0] = pages_ref[1]


def on_device(queries, new_keys, new_values, cache_keys, cache_values, hist_len, page_owner, out_weight):
    members = lax.axis_size("ctx")
    groups = lax.axis_size("tp")
    page, requests, width = queries.shape
    history = cache_keys.shape[1]
    heads = width // HD
    turn = page * members
    chunk = turn // 2
    owners = members // requests
    share_rows = turn // groups
    columns = out_weight.shape[1]
    vmem = pl.BlockSpec(memory_space=pltpu.VMEM)
    anywhere = pl.BlockSpec(memory_space=pl.ANY)
    bf16, f32 = jnp.bfloat16, jnp.float32
    dma = pltpu.SemaphoreType.DMA
    full, pages = pl.pallas_call(
        functools.partial(kernel, members, groups),
        out_shape=(
            jax.ShapeDtypeStruct((requests, share_rows, columns), f32),
            jax.ShapeDtypeStruct((2, *new_keys.shape), bf16),
        ),
        in_specs=[anywhere] * 8,
        out_specs=[vmem, vmem],
        scratch_shapes=[
            pltpu.VMEM(queries.shape, bf16),
            pltpu.SMEM(hist_len.shape, jnp.int32),
            pltpu.SMEM(page_owner.shape, jnp.int32),
            pltpu.VMEM((2 * history + HD, HD), bf16),
            pltpu.VMEM((2 * history + HD, HD), bf16),
            pltpu.VMEM((requests, *out_weight.shape), bf16),
            pltpu.VMEM((requests, page * heads, HD), f32),
            pltpu.VMEM((HD, HD), f32),
            pltpu.VMEM((members, requests, page * heads, HD), bf16),
            pltpu.VMEM((members, 2, *new_keys.shape), bf16),
            pltpu.VMEM((chunk * heads, 2 * history), f32),
            pltpu.VMEM((chunk * heads, 2 * HD), f32),
            pltpu.VMEM((chunk * heads, HD), f32),
            pltpu.VMEM((chunk * heads, HD), f32),
            pltpu.VMEM((owners, chunk, HD), bf16),
            pltpu.VMEM((owners, 1, HD), f32),
            pltpu.VMEM((owners, chunk, HD), bf16),
            pltpu.VMEM((owners, 1, HD), f32),
            pltpu.VMEM((heads, turn, HD), bf16),
            pltpu.VMEM((groups, requests, share_rows, columns), bf16),
            pltpu.VMEM((groups, requests, share_rows, columns), bf16),
            dma((8,)),
            dma((4,)),
            dma((4,)),
            dma(()),
            dma((members // 4,)),
            dma(()),
            dma((2,)),
            dma(()),
            dma(()),
            dma(()),
            dma(()),
            dma(()),
            dma(()),
            dma(()),
            dma(()),
            dma(()),
            dma(()),
        ],
        compiler_params=pltpu.CompilerParams(collective_id=0, has_side_effects=True),
    )(queries, new_keys, new_values, cache_keys, cache_values, hist_len, page_owner, out_weight)
    pages_shape = jax.ShapeDtypeStruct((1, *new_keys.shape), bf16)
    return pl.pallas_call(
        finish,
        out_shape=(jax.ShapeDtypeStruct((share_rows, requests, columns), bf16), pages_shape, pages_shape),
        in_specs=[vmem, vmem],
        out_specs=[vmem, vmem, vmem],
    )(full, pages)


def solution(mesh):
    return jax.shard_map(
        on_device,
        mesh=mesh,
        in_specs=(
            P("ctx", None, "tp"),
            P(None, "ctx", "tp"),
            P(None, "ctx", "tp"),
            P(None, "ctx", "tp"),
            P(None, "ctx", "tp"),
            P(),
            P(),
            P("tp", "ctx"),
        ),
        out_specs=(P("tp", None, "ctx"), P("ctx", None, None, "tp"), P("ctx", None, None, "tp")),
        check_vma=False,
    )
```

```python
import functools
import math

import jax
import jax.numpy as jnp
from jax import lax
from jax.experimental import pallas as pl
from jax.experimental.pallas import tpu as pltpu
from jax.sharding import PartitionSpec as P

HD = 128
FLOOR = -1e30
KEY_BLOCK = 4096
MESH = pl.DeviceIdType.MESH


def kernel(
    members,
    groups,
    q_hbm,
    nk_hbm,
    nv_hbm,
    ck_ref,
    cv_ref,
    hist_hbm,
    owner_hbm,
    w_ref,
    out_ref,
    pages_ref,
    q_ref,
    hist_ref,
    owner_ref,
    kbuf,
    vbuf,
    wbuf,
    qtmp,
    ktail,
    qall,
    kvall,
    scores,
    acc,
    ready,
    lse,
    osend,
    lsend,
    orecv,
    lrecv,
    abuf,
    psend,
    precv,
    load_sem,
    chip_send,
    chip_recv,
    z_send,
    z_recv,
    q_send,
    q_recv,
    page_send,
    page_recv,
    o_send,
    o_recv,
    l_send,
    l_recv,
    f_send,
    f_recv,
    p_send,
    p_recv,
):
    me = lax.axis_index("ctx")
    mine = lax.axis_index("tp")
    requests, history = ck_ref.shape[:2]
    page = q_hbm.shape[0]
    heads = q_hbm.shape[2] // HD
    turn = page * members
    chunk = turn // 2
    rows = chunk * heads
    half_size = history // 2
    owners = members // requests
    near = members // 2
    quarter = turn // groups // 2
    share_rows = turn // groups
    tail = kbuf.shape[0] - 2 * history
    factor = math.log2(math.e) / math.sqrt(HD)

    r = lax.rem(me, 2)
    other = 1 - r
    partner = me + 1 - 2 * r
    cell_size = 4
    depth = members // cell_size
    across = me + 2 - 4 * lax.rem(me // 2, 2)
    diagonal = across + 1 - 2 * r
    own = me // 2
    side = lax.rem(own, 2)
    level = own // 2

    load_k = pltpu.make_async_copy(ck_ref.at[r], kbuf.at[pl.ds(0, history)], load_sem.at[0])
    load_v = pltpu.make_async_copy(cv_ref.at[r], vbuf.at[pl.ds(0, history)], load_sem.at[1])
    load_w = pltpu.make_async_copy(w_ref, wbuf.at[r], load_sem.at[2])
    load_q = pltpu.make_async_copy(q_hbm, q_ref, load_sem.at[3])
    load_pages = (
        pltpu.make_async_copy(nk_hbm, kvall.at[me, 0], load_sem.at[4]),
        pltpu.make_async_copy(nv_hbm, kvall.at[me, 1], load_sem.at[5]),
    )
    load_hist = pltpu.make_async_copy(hist_hbm, hist_ref, load_sem.at[6])
    load_owner = pltpu.make_async_copy(owner_hbm, owner_ref, load_sem.at[7])
    load_q.start()

    barrier = pltpu.get_barrier_semaphore()

    def greet(**device):
        pl.semaphore_signal(barrier, inc=1, device_id=device, device_id_type=MESH)

    def by_distance(k):
        step = (k + 1) // 2
        return lax.rem(k, 2) * step + (1 - lax.rem(k, 2)) * (depth - step)

    def greet_z(k, c):
        greet(ctx=lax.rem(me + cell_size * by_distance(depth - k), members))
        return c

    def greet_tp(k, c):
        for j in range(requests):
            greet(ctx=me - r + j, tp=lax.rem(mine + k, groups))
        return c

    lax.fori_loop(1, depth, greet_z, 0)
    for cell in (partner, across, diagonal):
        greet(ctx=cell)
    lax.fori_loop(1, groups, greet_tp, 0)
    for copy in (*load_pages, load_hist, load_owner, load_k, load_v, load_w):
        copy.start()
    load_q.wait()

    for t in range(page):
        row = q_ref[t].astype(jnp.float32)
        for h in range(heads):
            for s in range(requests):
                qtmp[s, pl.ds(t * heads + h, 1), :] = row[s : s + 1, h * HD : (h + 1) * HD]
    def slot_of(device):
        return lax.rem(device // 2, 2) * near + device // 4 * 2 + lax.rem(device, 2)

    qall[slot_of(me), 0] = qtmp[r].astype(qall.dtype)
    qall[slot_of(me), 1] = qtmp[other].astype(qall.dtype)
    pl.semaphore_wait(barrier, depth - 1 + cell_size - 1 + requests * (groups - 1))

    def remote(src, dst, send_sem, recv_sem, **device):
        return pltpu.make_async_remote_copy(
            src_ref=src, dst_ref=dst, send_sem=send_sem, recv_sem=recv_sem, device_id=device, device_id_type=MESH
        )

    def landed(ref, sem):
        pltpu.make_async_copy(ref, ref, sem).wait()

    def query_to(peer, source):
        block = qall.at[slot_of(source)]
        return remote(block, block, z_send, z_recv.at[source // cell_size], ctx=peer)

    def send_query(k, c):
        query_to(lax.rem(me + cell_size * by_distance(depth - k), members), me).start()
        return c

    lax.fori_loop(1, depth, send_query, 0)

    def pass_on(source):
        slot = slot_of(source)
        for part, target, chunk_id in ((0, across, 1), (1, diagonal, 1), (1, partner, 0)):
            remote(qall.at[slot, part], qall.at[slot, 0], q_send, q_recv.at[chunk_id], ctx=target).start()

    pass_on(me)

    history_slab = pl.ds(history, history)
    give_k = remote(ck_ref.at[other], kbuf.at[history_slab], chip_send.at[0], chip_recv.at[0], ctx=partner)
    give_v = remote(cv_ref.at[other], vbuf.at[history_slab], chip_send.at[1], chip_recv.at[1], ctx=partner)
    give_w = remote(w_ref, wbuf.at[r], chip_send.at[2], chip_recv.at[2], ctx=partner)
    give_page = remote(kvall.at[me], kvall.at[me], chip_send.at[3], chip_recv.at[3], ctx=partner)
    for copy in load_pages:
        copy.wait()
    give_page.start()
    give_k.start()
    give_v.start()

    def relay(k, c):
        source = lax.rem(me + cell_size * by_distance(k), members)
        query_to(me, source).wait_recv()
        pass_on(source)
        return c

    lax.fori_loop(1, depth, relay, 0)
    give_w.start()

    give_page.wait_recv()
    for source, target in ((0, kbuf), (1, vbuf)):
        ktail[...] = jnp.zeros_like(ktail)
        for j in range(2):
            ktail[pl.ds(j * page, page), :] = kvall[me - r + j, source, r].astype(jnp.float32)
        target[pl.ds(2 * history, tail), :] = ktail[...].astype(target.dtype)

    ones = jnp.ones((KEY_BLOCK, HD), jnp.bfloat16)
    row_index = lax.broadcasted_iota(jnp.int32, (rows, tail), 0) // heads
    row_token = row_index // quarter * (2 * quarter) + lax.rem(row_index, quarter)
    tail_lane = lax.broadcasted_iota(jnp.int32, (rows, tail), 1)
    token_row = lax.broadcasted_iota(jnp.int32, (chunk, HD), 0)
    token_lane = lax.broadcasted_iota(jnp.int32, (chunk, HD), 1)
    lane = lax.broadcasted_iota(jnp.int32, (1, KEY_BLOCK), 1)

    def bias_of(device, offset):
        slot = lane + offset
        low = hist_ref[r] - device * half_size
        high = hist_ref[r] - (2 * members - 1 - device) * half_size + half_size
        return jnp.where(slot < jnp.where(slot < half_size, low, high), 0.0, FLOOR)

    dot_nt = functools.partial(
        lax.dot_general,
        dimension_numbers=(((1,), (1,)), ((), ())),
        preferred_element_type=jnp.float32,
    )

    steps = 2 * history // KEY_BLOCK

    def attend(i, c):
        which = lax.rem(side + i, 2)
        first = which * near

        @pl.when(i == 0)
        def _():
            load_k.wait()
            landed(qall.at[pl.ds(0, depth), 0], q_recv.at[0])

        @pl.when(i == 1)
        def _():
            landed(qall.at[pl.ds(0, near), 0], q_recv.at[1])

        queries = qall[pl.ds(first, near), 0].reshape(rows, HD)

        def score(b, peak):
            offset = pl.multiple_of(b * KEY_BLOCK, KEY_BLOCK)

            @pl.when((i == 0) & (offset == history))
            def _():
                give_k.wait_recv()

            given = offset // history
            block = dot_nt(queries, kbuf[pl.ds(offset, KEY_BLOCK), :])
            block = block + bias_of(me + (partner - me) * given, offset - history * given)
            scores[:, pl.ds(offset, KEY_BLOCK)] = block
            for p in range(KEY_BLOCK // HD):
                peak = jnp.maximum(peak, block[:, p * HD : (p + 1) * HD])
            return peak

        last = dot_nt(queries, kbuf[2 * history :, :])
        visible = (tail_lane < 2 * page) & (tail_lane + 2 * page * own <= row_token + which * quarter)
        last = jnp.where(visible, last, FLOOR)
        peak = jnp.max(lax.fori_loop(0, steps, score, last), axis=1, keepdims=True)
        weights = jnp.exp2((last - peak) * factor).astype(jnp.bfloat16)
        values = jnp.concatenate([vbuf[2 * history :, :], ones[:tail]], axis=1)
        acc[...] = jnp.dot(weights, values, preferred_element_type=jnp.float32)

        @pl.when(i == 0)
        def _():
            load_v.wait()
            give_v.wait_recv()

        def weigh(b, c):
            offset = pl.multiple_of(b * KEY_BLOCK, KEY_BLOCK)
            weights = jnp.exp2((scores[:, pl.ds(offset, KEY_BLOCK)] - peak) * factor).astype(jnp.bfloat16)
            values = jnp.concatenate([vbuf[pl.ds(offset, KEY_BLOCK), :], ones], axis=1)
            acc[...] += jnp.dot(weights, values, preferred_element_type=jnp.float32)
            return c

        lax.fori_loop(0, steps, weigh, 0)
        total = acc[:, HD:]
        lse[...] = peak * factor + jnp.log2(total)
        ready[...] = acc[:, :HD] / total

        def pack(h):
            picked = pl.ds(h, chunk, stride=heads)
            target = 2 * h + 1 - which
            osend[target] = ready[picked, :].astype(osend.dtype)
            lsend[target] = jnp.sum(jnp.where(token_row == token_lane, lse[picked, :], 0.0), axis=0, keepdims=True)

        def send_piece(h):
            target = 2 * h + 1 - which

            @pl.when(target != own)
            def _():
                remote(osend.at[target], orecv.at[own], o_send, o_recv, ctx=requests * target + r).start()
                remote(lsend.at[target], lrecv.at[own], l_send, l_recv, ctx=requests * target + r).start()

        def turned(k):
            return lax.rem(k + level, heads)

        def piece(k, c):
            pack(turned(k))
            send_piece(turned(k - 1))
            return c

        pack(turned(0))
        lax.fori_loop(1, heads, piece, 0)
        send_piece(turned(heads - 1))
        return c

    load_hist.wait()
    load_owner.wait()
    lax.fori_loop(0, 2, attend, 0)

    def send_page(k, c):
        peer = lax.rem(me + k, members)

        @pl.when(peer != partner)
        def _():
            remote(kvall.at[me], kvall.at[me], page_send, page_recv, ctx=peer).start()

        return c

    lax.fori_loop(1, members, send_page, 0)

    orecv[own] = osend[own]
    lrecv[own] = lsend[own]
    landed(lrecv.at[pl.ds(0, owners - 1)], l_recv)
    levels = lrecv[...].reshape(owners, HD)
    levels = jnp.concatenate([levels, jnp.full((HD - owners, HD), FLOOR, jnp.float32)], axis=0)
    levels = levels.T[:chunk]
    share = jnp.exp2(levels - jnp.max(levels, axis=1, keepdims=True))
    share = share / jnp.sum(share, axis=1, keepdims=True)
    landed(orecv.at[pl.ds(0, owners - 1)], o_recv)
    done = jnp.zeros((chunk, HD), jnp.float32)
    for s in range(owners):
        done = done + share[:, s : s + 1] * orecv[s].astype(jnp.float32)
    place = abuf.at[level, pl.ds(pl.multiple_of((1 - side) * chunk, chunk), chunk)]
    place[...] = done.astype(abuf.dtype)

    def send_finished(k, c):
        remote(place, place, f_send, f_recv, ctx=lax.rem(me + requests * k, members)).start()
        return c

    lax.fori_loop(1, owners, send_finished, 0)

    landed(kvall.at[pl.ds(0, members - 2)], page_recv)
    for s in range(requests):
        source = jnp.int32(0)
        for b in range(members):
            source = jnp.maximum(source, jnp.where(owner_ref[s, b] == me, b, 0))
        for kind in range(2):
            pages_ref[kind, s] = kvall[source, kind, s]
    load_w.wait()
    give_w.wait_recv()

    flat = abuf.reshape(owners, chunk, HD)
    landed(flat.at[pl.ds(0, owners - 1)], f_recv)
    rows_in = jnp.concatenate([abuf[h] for h in range(heads)], axis=1)
    def project(j, c):
        part = jnp.dot(rows_in, wbuf[j], preferred_element_type=jnp.float32)
        for g in range(groups):
            halves = [part[y * chunk + g * quarter : y * chunk + (g + 1) * quarter] for y in range(2)]
            psend[g, j] = jnp.concatenate(halves, axis=0).astype(psend.dtype)

        def send_part(k, c):
            peer = lax.rem(mine + k, groups)
            remote(psend.at[peer, j], precv.at[mine, r], p_send, p_recv, ctx=me - r + j, tp=peer).start()
            return c

        lax.fori_loop(1, groups, send_part, 0)
        return c

    lax.fori_loop(0, requests, project, 0)
    remote(psend.at[mine, other], precv.at[mine, r], p_send, p_recv, ctx=partner).start()
    precv[mine, r] = psend[mine, r]
    flat_parts = precv.reshape(requests * groups, share_rows, precv.shape[3])
    landed(flat_parts.at[pl.ds(0, requests * groups - 1)], p_recv)
    full = precv[0].astype(jnp.float32)
    for g in range(1, groups):
        full = full + precv[g].astype(jnp.float32)
    out_ref[...] = full

    for give in (give_k, give_v, give_w, give_page):
        give.wait_send()
    landed(qall.at[pl.ds(0, depth - 1)], z_send)
    landed(qall.at[pl.ds(0, 3 * depth), 0], q_send)
    landed(kvall.at[pl.ds(0, members - 2)], page_send)
    landed(orecv.at[pl.ds(0, owners - 1)], o_send)
    landed(lrecv.at[pl.ds(0, owners - 1)], l_send)
    landed(flat.at[pl.ds(0, owners - 1)], f_send)
    landed(flat_parts.at[pl.ds(0, requests * groups - 1)], p_send)


def finish(full_ref, pages_ref, attended_ref, keys_ref, values_ref):
    parts = [full_ref[r] for r in range(full_ref.shape[0])]
    attended_ref[...] = jnp.stack(parts, axis=1).astype(attended_ref.dtype)
    keys_ref[0] = pages_ref[0]
    values_ref[0] = pages_ref[1]


def on_device(queries, new_keys, new_values, cache_keys, cache_values, hist_len, page_owner, out_weight):
    members = lax.axis_size("ctx")
    groups = lax.axis_size("tp")
    page, requests, width = queries.shape
    history = cache_keys.shape[1]
    heads = width // HD
    turn = page * members
    chunk = turn // 2
    owners = members // requests
    share_rows = turn // groups
    columns = out_weight.shape[1]
    vmem = pl.BlockSpec(memory_space=pltpu.VMEM)
    anywhere = pl.BlockSpec(memory_space=pl.ANY)
    bf16, f32 = jnp.bfloat16, jnp.float32
    dma = pltpu.SemaphoreType.DMA
    full, pages = pl.pallas_call(
        functools.partial(kernel, members, groups),
        out_shape=(
            jax.ShapeDtypeStruct((requests, share_rows, columns), f32),
            jax.ShapeDtypeStruct((2, *new_keys.shape), bf16),
        ),
        in_specs=[anywhere] * 8,
        out_specs=[vmem, vmem],
        scratch_shapes=[
            pltpu.VMEM(queries.shape, bf16),
            pltpu.SMEM(hist_len.shape, jnp.int32),
            pltpu.SMEM(page_owner.shape, jnp.int32),
            pltpu.VMEM((2 * history + HD, HD), bf16),
            pltpu.VMEM((2 * history + HD, HD), bf16),
            pltpu.VMEM((requests, *out_weight.shape), bf16),
            pltpu.VMEM((requests, page * heads, HD), f32),
            pltpu.VMEM((HD, HD), f32),
            pltpu.VMEM((members, requests, page * heads, HD), bf16),
            pltpu.VMEM((members, 2, *new_keys.shape), bf16),
            pltpu.VMEM((chunk * heads, 2 * history), f32),
            pltpu.VMEM((chunk * heads, 2 * HD), f32),
            pltpu.VMEM((chunk * heads, HD), f32),
            pltpu.VMEM((chunk * heads, HD), f32),
            pltpu.VMEM((owners, chunk, HD), bf16),
            pltpu.VMEM((owners, 1, HD), f32),
            pltpu.VMEM((owners, chunk, HD), bf16),
            pltpu.VMEM((owners, 1, HD), f32),
            pltpu.VMEM((heads, turn, HD), bf16),
            pltpu.VMEM((groups, requests, share_rows, columns), bf16),
            pltpu.VMEM((groups, requests, share_rows, columns), bf16),
            dma((8,)),
            dma((4,)),
            dma((4,)),
            dma(()),
            dma((members // 4,)),
            dma(()),
            dma((2,)),
            dma(()),
            dma(()),
            dma(()),
            dma(()),
            dma(()),
            dma(()),
            dma(()),
            dma(()),
            dma(()),
            dma(()),
        ],
        compiler_params=pltpu.CompilerParams(collective_id=0, has_side_effects=True),
    )(queries, new_keys, new_values, cache_keys, cache_values, hist_len, page_owner, out_weight)
    pages_shape = jax.ShapeDtypeStruct((1, *new_keys.shape), bf16)
    return pl.pallas_call(
        finish,
        out_shape=(jax.ShapeDtypeStruct((share_rows, requests, columns), bf16), pages_shape, pages_shape),
        in_specs=[vmem, vmem],
        out_specs=[vmem, vmem, vmem],
    )(full, pages)


def solution(mesh):
    return jax.shard_map(
        on_device,
        mesh=mesh,
        in_specs=(
            P("ctx", None, "tp"),
            P(None, "ctx", "tp"),
            P(None, "ctx", "tp"),
            P(None, "ctx", "tp"),
            P(None, "ctx", "tp"),
            P(),
            P(),
            P("tp", "ctx"),
        ),
        out_specs=(P("tp", None, "ctx"), P("ctx", None, None, "tp"), P("ctx", None, None, "tp")),
        check_vma=False,
    )
```
